256 devices in a mesh: dp: 16 (over y_hi, x, core), tm: 16 (over y_lo, z).
Axes of the slice: x: 4, y: 4 (y_hi: 2, y_lo: 2; y = y_hi * 2 + y_lo), z: 8, core: 2. Of those that a mesh axis runs over, the one named last changes fastest.
Arguments:
- query_rows: bfloat16 [16, 3584, 1024], P('dp', 'tm'), may hold values from -6 to 6
- key_rows: bfloat16 [16, 3584, 1024], P('dp', 'tm'), may hold values from -6 to 6
- value_rows: bfloat16 [16, 3584, 1024], P('dp', 'tm'), may hold values from -6 to 6
- head_scale: float32 [16], replicated, may hold values from 2 to 16
- out_proj: bfloat16 [1024, 1536], replicated, may hold values from -0.1875 to 0.1875
- conv_taps: float32 [31, 1536], replicated, may hold values from -1 to 1
- router: bfloat16 [1536, 16], replicated, may hold values from -0.15625 to 0.15625
- expert_in: bfloat16 [16, 2048, 1536], P('dp', 'tm'), may hold values from -0.15625 to 0.15625
- expert_out: bfloat16 [16, 2048, 1536], P('dp', 'tm'), may hold values from -0.125 to 0.125
- lengths: int32 [16, 4], P('dp'), may hold values from 1 to 2688, 3584 in all within a row
- routes: int32 [16, 3584, 2], P('dp', 'tm'), may hold values from 0 to 15, all different within a row; in each aligned block of 224 rows (0 to 223, 224 to 447, ..., all dimensions but the last counted through in order) at most 42 rows name the same one
Outputs:
- block_out: bfloat16 [16, 3584, 1536], P('dp', 'tm')
The draws below stay inside these ranges and needn't reach their ends.
Inputs may be any that keep to these rules, and one draw needn't show every extreme that they name: Every length is at least 1, the 4 lengths of a pack sum to 3584, and the largest of each pack is exactly 2688. `routes`: the 2 experts of a frame differ. Among the 224 frames of one block (frames j * 224 to (j + 1) * 224 - 1 of a pack), no expert is named by more than 42 frames, and in some block some expert is named by exactly 42. Every expert is named somewhere.
All inputs are finite; a program needn't handle non-finite values.
Results may differ from the reference program's by a relative error of at most 0.0099.
Values may be sent and summed in bfloat16 or wider, within the bound.
A program may use at most 128 MiB of HBM per device.

```python
import math
import jax
import jax.numpy as jnp
import numpy as np
from jax import lax

D = 1536
HEADS = 16
HEAD_DIM = 64
KERNEL = 31
HALF = 15
FF_E = 2048
TOPK = 2
RECS = 4
ROWS = 224
EXPERTS = 16
PACKS = 16
FRAMES = 3584
MOST = 2688
CAP = 42
N_TM = 16


def shard_levels(own_key, extent, cuts, low, top_value):
    loudness, own = 1.0, jax.random.fold_in(own_key, 6)
    for position, parts in cuts:
        draws = jnp.exp(jax.random.uniform(jax.random.fold_in(own, position), (parts,), jnp.float32, low / len(cuts), top_value / len(cuts)))
        loudness = loudness * jnp.repeat(draws, extent[position] // parts).reshape([-1 if axis == position else 1 for axis in range(len(extent))])
    return loudness


def length_profile(amount, total, most, skew):
    loads = [(1 << 20) // math.isqrt(grade ** skew) + 1 for grade in range(2, amount + 1)]
    rest, holding = total - most - (amount - 1), [1] * (amount - 1)
    while rest > 0:
        candidates = [i for i in range(amount - 1) if holding[i] < most]
        whole, left = sum([loads[i] for i in candidates]), rest
        for i in candidates:
            addition = min(most - holding[i], max(1, left * loads[i] // whole), rest)
            holding[i] = holding[i] + addition
            rest = rest - addition
    return np.array([most] + holding)


def ragged_sizes(own_key, number_of, total, limit, slope):
    if number_of == 2:
        one = jax.random.randint(own_key, (), max(1, total - limit), min(limit, total - 1) + 1)
        return jnp.stack([one, total - one])
    sizes = jnp.asarray(length_profile(number_of, total, limit, slope), jnp.int32)
    twos = (number_of - 1) // 2
    donor, receiver = sizes[1:1 + 2 * twos:2], sizes[2:2 + 2 * twos:2]
    room = jnp.minimum(donor - 1, limit - receiver)
    passed = jax.random.randint(jax.random.fold_in(own_key, 1), (twos,), 0, 1 << 20) % (room + 1)
    sizes = sizes.at[1:1 + 2 * twos:2].set(donor - passed).at[2:2 + 2 * twos:2].set(receiver + passed)
    return sizes[jax.random.permutation(jax.random.fold_in(own_key, 2), number_of)]


def deal_out(key, own, number, rows, count, top, bound, slope):
    order = jax.random.permutation(key, count)
    heavy_load, ordinary = shares(count, rows * top, bound, slope, True), shares(count, rows * top, bound, slope, False)
    places = jnp.arange(count)

    def named(sizes, offset_by):
        used = int((sizes > 0).sum())
        fixed = max(1, used // 4)
        shifted = fixed + (places - fixed + offset_by * (used - fixed)) % max(1, count - fixed)
        return jnp.zeros((count,), jnp.int32).at[order[jnp.where(places < fixed, places, shifted)]].set(jnp.asarray(sizes, jnp.int32))

    sizes = jnp.where(number % 4 == 0, named(heavy_load, number // 4), named(ordinary, number - number // 4 - 1))
    mixed = jax.random.permutation(jax.random.fold_in(own, 3), count)
    source_of, receiver = mixed[0:count // 2 * 2:2], mixed[1:count // 2 * 2:2]
    room = jnp.minimum(sizes[source_of] - 1, bound - sizes[receiver]) // 2
    room = jnp.where((source_of == order[0]) | (receiver == order[0]) | (sizes[receiver] == 0), 0, jnp.maximum(room, 0))
    shifted = jax.random.randint(jax.random.fold_in(own, 4), (count // 2,), 0, 1 << 20) % (room + 1)
    sizes = sizes.at[source_of].add(-shifted).at[receiver].add(shifted)
    items = jnp.searchsorted(jnp.cumsum(sizes), jnp.arange(rows * top), side="right").astype(jnp.int32)
    table = items.reshape(top, rows).T
    table = table[jax.random.permutation(jax.random.fold_in(own, 1), rows)]
    offset_by = jax.random.randint(jax.random.fold_in(own, 2), (rows, 1), 0, top)
    return jnp.take_along_axis(table, (jnp.arange(top)[None, :] + offset_by) % top, axis=1)


def shares(count, total, reach, slope, full):
    loads = [(1 << 20) // math.isqrt(standing ** slope) + 1 for standing in range(1, count + 1)]
    largest = reach if full else min(reach, max(-(-total // count), total * loads[0] // sum(loads)))
    least = 1 if total - largest >= count - 1 else 0
    holding, rest = [largest] + [least] * (count - 1), total - largest - least * (count - 1)
    while rest > 0:
        movable = [i for i in range(1, count) if holding[i] < largest] or [i for i in range(1, count) if holding[i] < reach]
        mass, left = sum([loads[i] for i in movable]), rest
        for i in movable:
            more = min(reach - holding[i], max(1, left * loads[i] // mass), rest)
            holding[i] = holding[i] + more
            rest = rest - more
    return np.array(holding)


def gaussian(own_key, dims, deviation, most, shards=(), kind=jnp.bfloat16):
    values = jax.random.normal(own_key, dims, jnp.float32) * deviation
    if len(shards) > 0:
        values = shard_levels(own_key, dims, shards, -0.22, 0.18) * values
    return jnp.clip(values, min=-most, max=most).astype(kind)


def setup_inputs(seed: int = 0) -> dict:
    keys = jax.random.split(jax.random.key(seed), 12)
    query_rows = gaussian(keys[0], (PACKS, FRAMES, HEADS * HEAD_DIM), 1.0, 6.0, ((0, 16), (1, 16)))
    key_rows = gaussian(keys[1], (PACKS, FRAMES, HEADS * HEAD_DIM), 1.0, 6.0, ((0, 16), (1, 16)))
    value_rows = gaussian(keys[2], (PACKS, FRAMES, HEADS * HEAD_DIM), 1.0, 6.0, ((0, 16), (1, 16)))
    head_scale = jnp.clip(jnp.exp(jax.random.uniform(keys[3], (HEADS,), jnp.float32, math.log(2.0), math.log(16.0))), 2.0, 16.0)
    out_proj = gaussian(keys[4], (HEADS * HEAD_DIM, D), (HEADS * HEAD_DIM) ** -0.5, 0.1875)
    conv_taps = gaussian(keys[5], (KERNEL, D), KERNEL ** -0.5, 1.0, (), jnp.float32)
    router = gaussian(keys[6], (D, EXPERTS), D ** -0.5, 0.15625)
    expert_in = gaussian(keys[7], (EXPERTS, FF_E, D), D ** -0.5, 0.15625, ((0, 16), (1, 16)))
    expert_out = gaussian(keys[8], (EXPERTS, FF_E, D), FF_E ** -0.5, 0.125, ((0, 16), (1, 16)))
    lengths = jax.vmap(lambda own: ragged_sizes(own, RECS, FRAMES, MOST, 2))(jax.random.split(keys[9], PACKS)).reshape((PACKS, RECS)).astype(jnp.int32)
    routes_keys = jax.random.split(jax.random.fold_in(keys[10], 1), PACKS * FRAMES // ROWS)
    routes_turns = jax.random.permutation(jax.random.fold_in(keys[10], 3), PACKS * FRAMES // ROWS)
    routes = jax.vmap(lambda own, number: deal_out(jax.random.fold_in(keys[10], 2), own, number, ROWS, EXPERTS, TOPK, CAP, 2))(routes_keys, routes_turns).reshape((PACKS, FRAMES, TOPK))
    return {"query_rows": query_rows, "key_rows": key_rows, "value_rows": value_rows, "head_scale": head_scale, "out_proj": out_proj, "conv_taps": conv_taps, "router": router, "expert_in": expert_in, "expert_out": expert_out, "lengths": lengths, "routes": routes}


def layer_norm(values):
    average = lax.optimization_barrier(jnp.mean(values, axis=-1, keepdims=True))
    centered = values - average
    spread = lax.optimization_barrier(jnp.mean(centered * centered, axis=-1, keepdims=True))
    return centered * lax.rsqrt(spread + 1e-05)

def unit_heads(rows):
    lifted = rows.astype(jnp.float32).reshape(rows.shape[0], HEADS, HEAD_DIM)
    factor = lax.rsqrt(lax.optimization_barrier(jnp.sum(lifted * lifted, axis=-1, keepdims=True)) + 1e-06)
    return (lifted * factor).astype(jnp.bfloat16)

def recording_of(positions, pack_lengths):
    bounds = jnp.cumsum(pack_lengths).astype(jnp.int32)[:RECS - 1]
    return lax.optimization_barrier(jnp.sum((positions[:, None] >= bounds[None, :]).astype(jnp.int32), axis=1)).astype(jnp.int32)

def attend_pack(query_rows, key_rows, value_rows, pack_lengths, head_scale):
    frames = jnp.arange(FRAMES, dtype=jnp.int32)
    labels = recording_of(frames, pack_lengths)
    query_unit = unit_heads(query_rows)
    key_unit = unit_heads(key_rows).astype(jnp.float32)
    value_heads = value_rows.astype(jnp.float32).reshape(FRAMES, HEADS, HEAD_DIM)
    block = math.gcd(FRAMES, 512)

    def one_block(first):
        query_block = lax.dynamic_slice_in_dim(query_unit, first, block, 0).astype(jnp.float32)
        query_labels = lax.dynamic_slice_in_dim(labels, first, block, 0)
        scores = jnp.einsum('qhd,khd->hqk', query_block, key_unit)
        inside = (query_labels[:, None] == labels[None, :])[None]
        weights = jnp.where(inside, jnp.exp(head_scale[:, None, None] * (scores - 1.0)), 0.0)
        masses = lax.optimization_barrier(jnp.sum(weights, axis=-1))
        rounded = lax.optimization_barrier(weights.astype(jnp.bfloat16)).astype(jnp.float32)
        summed = jnp.einsum('hqk,khd->qhd', rounded, value_heads)
        return (summed / jnp.transpose(masses)[:, :, None]).reshape(block, HEADS * HEAD_DIM).astype(jnp.bfloat16)
    starts = jnp.arange(FRAMES // block, dtype=jnp.int32) * block
    return lax.map(one_block, starts).reshape(FRAMES, HEADS * HEAD_DIM)

def conv_pack(normed, pack_lengths, conv_taps):
    labels = recording_of(jnp.arange(FRAMES, dtype=jnp.int32), pack_lengths)
    padded = jnp.pad(normed, ((HALF, HALF), (0, 0)))
    padded_labels = recording_of(jnp.arange(-HALF, FRAMES + HALF, dtype=jnp.int32), pack_lengths)
    total = jnp.zeros((FRAMES, D), jnp.float32)
    for offset in range(KERNEL):
        same = (padded_labels[offset:offset + FRAMES] == labels)[:, None]
        term = conv_taps[offset][None, :] * padded[offset:offset + FRAMES].astype(jnp.float32)
        total = total + jnp.where(same, term, 0.0)
    return total

def reference(query_rows, key_rows, value_rows, head_scale, out_proj, conv_taps, router, expert_in, expert_out, lengths, routes):
    attended = lax.map(lambda items: attend_pack(items[0], items[1], items[2], items[3], head_scale), (query_rows, key_rows, value_rows, lengths))
    first = jnp.dot(attended.reshape(PACKS * FRAMES, HEADS * HEAD_DIM), out_proj, preferred_element_type=jnp.float32)
    normed = layer_norm(first).astype(jnp.bfloat16)
    convolved = lax.map(lambda items: conv_pack(items[0], items[1], conv_taps), (normed.reshape(PACKS, FRAMES, D), lengths))
    second = first + jax.nn.silu(convolved.reshape(PACKS * FRAMES, D))
    mixed_in = layer_norm(second).astype(jnp.bfloat16)
    logits = jnp.dot(mixed_in, router, preferred_element_type=jnp.float32)
    flat_routes = routes.reshape(PACKS * FRAMES, TOPK)
    chosen = jnp.exp(jnp.take_along_axis(logits, flat_routes, axis=1))
    gates = chosen / lax.optimization_barrier(jnp.sum(chosen, axis=1, keepdims=True))
    blocks = PACKS * N_TM
    block_routes = flat_routes.reshape(blocks, ROWS, TOPK)
    picks = lax.optimization_barrier(jnp.sum((block_routes[:, :, :, None] == jnp.arange(EXPERTS, dtype=jnp.int32)).astype(jnp.int32), axis=2)).astype(jnp.int32)
    ranks = (jnp.cumsum(picks, axis=1) - picks).astype(jnp.int32)
    slot_rank = jnp.take_along_axis(ranks, block_routes, axis=2).astype(jnp.int32)
    block_ids = jnp.broadcast_to(jnp.arange(blocks, dtype=jnp.int32)[:, None, None], block_routes.shape)
    frame_ids = jnp.broadcast_to(jnp.arange(PACKS * FRAMES, dtype=jnp.int32).reshape(blocks, ROWS, 1), block_routes.shape)
    sentinel = PACKS * FRAMES
    table = jnp.full((EXPERTS, blocks, CAP), sentinel, jnp.int32).at[block_routes, block_ids, slot_rank].set(frame_ids)
    gate_table = jnp.zeros((EXPERTS, blocks, CAP), jnp.float32).at[block_routes, block_ids, slot_rank].set(gates.reshape(blocks, ROWS, TOPK))
    padded_in = jnp.concatenate([mixed_in, jnp.zeros((1, D), jnp.bfloat16)], axis=0)

    def one_expert(summed, items):
        frame_list, weights_in, weights_out, gate_rows = items
        frame_list = frame_list.reshape(-1)
        tokens = padded_in[frame_list]
        hidden = jax.nn.silu(jnp.dot(tokens, weights_in.T, preferred_element_type=jnp.float32)).astype(jnp.bfloat16)
        result = jnp.dot(hidden, weights_out, preferred_element_type=jnp.float32).astype(jnp.bfloat16)
        summed = summed.at[frame_list].add(gate_rows.reshape(-1)[:, None] * result.astype(jnp.float32), mode='drop')
        return (summed, None)
    mixture, _ = lax.scan(one_expert, jnp.zeros((PACKS * FRAMES, D), jnp.float32), (table, expert_in, expert_out, gate_table))
    return (second + 0.5 * mixture).astype(jnp.bfloat16).reshape(PACKS, FRAMES, D)
```

```python
import functools

import jax
import jax.numpy as jnp
from jax import lax
from jax.experimental import pallas as pl
from jax.experimental.pallas import tpu as pltpu
from jax.sharding import PartitionSpec as P

D = 1536
HEADS = 16
HEAD_DIM = 64
KERNEL = 31
HALF = 15
TOPK = 2
RECS = 4
EDGE = 16
CAP_PAD = 48
MESH = pl.DeviceIdType.MESH
BF = jnp.bfloat16
F32 = jnp.float32
VMEM_LIMIT = 60 * 1024 * 1024


def any_spec():
    return pl.BlockSpec(memory_space=pl.ANY)


def vmem_spec():
    return pl.BlockSpec(memory_space=pltpu.VMEM)


def smem_spec():
    return pl.BlockSpec(memory_space=pltpu.SMEM)


def dot(a, b, dims=((1,), (0,))):
    return lax.dot_general(a, b, (dims, ((), ())), preferred_element_type=F32)


def greet(axis, count):
    barrier = pltpu.get_barrier_semaphore()
    me = lax.axis_index(axis)
    for step in range(1, count):
        pl.semaphore_signal(
            barrier, inc=1, device_id={axis: lax.rem(me + step, count)}, device_id_type=MESH
        )


def greeted(total):
    pl.semaphore_wait(pltpu.get_barrier_semaphore(), total)


def spread(axis, count, source, target, send_sem, recv_sem, own_sem):
    me = lax.axis_index(axis)
    copies = []
    for step in range(1, count):
        peer = lax.rem(me + step, count)
        copy = pltpu.make_async_remote_copy(
            src_ref=source.at[peer],
            dst_ref=target.at[me],
            send_sem=send_sem.at[step - 1],
            recv_sem=recv_sem.at[step - 1],
            device_id={axis: peer},
            device_id_type=MESH,
        )
        copy.start()
        copies.append(copy)
    own = pltpu.make_async_copy(source.at[me], target.at[me], own_sem)
    own.start()
    copies.append(own)
    return copies


def low_lanes(shape):
    return lax.broadcasted_iota(jnp.int32, shape, 1) < HEAD_DIM


def pair_ones():
    row = lax.broadcasted_iota(jnp.int32, (128, 128), 0) // HEAD_DIM
    col = lax.broadcasted_iota(jnp.int32, (128, 128), 1) // HEAD_DIM
    return (row == col).astype(F32).astype(BF)


def unit_pair(tile, ones):
    square = tile * tile
    high = square.astype(BF)
    rest = (square - high.astype(F32)).astype(BF)
    total = dot(high, ones) + dot(rest, ones)
    return tile * lax.rsqrt(total + 1e-06)


def swap(tile):
    return pltpu.roll(tile, HEAD_DIM, 1)


def heads_kernel(count, q_ref, k_ref, v_ref, out_ref, pack, send_sem, recv_sem, own_sem):
    greet("tm", count)
    rows = q_ref.shape[0]
    part = rows // 2
    ones = pair_ones()
    low = low_lanes((rows, 128))
    low_part = low_lanes((part, 128))
    for pair in range(HEADS // 2):
        lanes = slice(128 * pair, 128 * pair + 128)
        q = unit_pair(q_ref[:, lanes].astype(F32), ones)
        k = unit_pair(k_ref[:, lanes].astype(F32), ones)
        pack[2 * pair, :rows, :] = jnp.where(low, q, swap(k)).astype(BF)
        pack[2 * pair + 1, :rows, :] = jnp.where(low, swap(q), k).astype(BF)
        upper = v_ref[:part, lanes].astype(F32)
        lower = v_ref[part:, lanes].astype(F32)
        pack[2 * pair, rows:, :] = jnp.where(low_part, upper, swap(lower)).astype(BF)
        pack[2 * pair + 1, rows:, :] = jnp.where(low_part, swap(upper), lower).astype(BF)
    greeted(count - 1)
    for copy in spread("tm", count, pack, out_ref, send_sem, recv_sem, own_sem):
        copy.wait()


TQ = 256
TK = 256


def attend_kernel(
    count, scale_ref, lengths_ref, in_ref, out_ref, qs, ks, vs, outs, key_label, own_label
):
    rows = in_ref.shape[1] * 2 // 3
    part = rows // 2
    frames = rows * count
    me = lax.axis_index("tm")
    scale = scale_ref[me] * 1.4426950408889634
    ends = [lengths_ref[0, 0]]
    for r in range(1, RECS):
        ends.append(ends[-1] + lengths_ref[0, r])
    low = low_lanes((rows, 128))
    low_part = low_lanes((part, 128))

    def unpack(block, carry):
        base = pl.multiple_of(block * rows, 32)
        tile = in_ref[block, :rows, :].astype(F32)
        qs[pl.ds(base, rows), :] = jnp.where(low, tile, 0.0).astype(BF)
        ks[pl.ds(base, rows), :] = swap(tile).astype(BF)
        values = in_ref[block, rows:, :].astype(F32)
        vs[pl.ds(base, part), :] = jnp.where(low_part, values, 1.0).astype(BF)
        vs[pl.ds(base + part, part), :] = jnp.where(low_part, swap(values), 1.0).astype(BF)
        return carry

    lax.fori_loop(0, count, unpack, 0)
    spot = lax.broadcasted_iota(jnp.int32, (8, frames), 1)
    key_label[...] = sum((spot >= ends[r]).astype(jnp.int32) for r in range(RECS - 1))
    outs[:EDGE, :] = jnp.zeros((EDGE, 128), BF)
    outs[EDGE + frames :, :] = jnp.zeros((EDGE, 128), BF)

    def one_block(step, carry):
        base = pl.multiple_of(step * TQ, TQ)
        last = base + (TQ - 1)
        first_key = jnp.int32(0)
        for r in range(RECS - 1):
            first_key = jnp.where(base >= ends[r], ends[r], first_key)
        end_key = ends[RECS - 1]
        for r in range(RECS - 2, -1, -1):
            end_key = jnp.where(last < ends[r], ends[r], end_key)
        place = base + lax.broadcasted_iota(jnp.int32, (TQ, 128), 0)
        own = sum((place >= ends[r]).astype(jnp.int32) for r in range(RECS - 1))
        own_label[...] = own
        query = qs[pl.ds(base, TQ), :]

        def one_key(tile, total):
            start = pl.multiple_of(tile * TK, TK)
            scores = dot(query, ks[pl.ds(start, TK), :], ((1,), (1,)))
            powers = jnp.exp2(scores * scale - scale)
            label = jnp.broadcast_to(key_label[0:1, pl.ds(start, TK)], (TQ, TK))
            wide = jnp.concatenate([own_label[...]] * (TK // 128), axis=1)
            weight = jnp.where(wide == label, powers, 0.0).astype(BF)
            return total + dot(weight, vs[pl.ds(start, TK), :])

        total = lax.fori_loop(
            first_key // TK, (end_key + TK - 1) // TK, one_key, jnp.zeros((TQ, 128), F32)
        )
        outs[pl.ds(EDGE + base, TQ), :] = (total / swap(total)).astype(BF)
        return carry

    lax.fori_loop(0, frames // TQ, one_block, 0)
    half = (rows + 2 * EDGE) // 2
    low_half = low_lanes((half, 128))

    def deal(block, carry):
        base = pl.multiple_of(block * rows, 32)
        upper = outs[pl.ds(base, half), :].astype(F32)
        lower = outs[pl.ds(base + half, half), :].astype(F32)
        out_ref[block] = jnp.where(low_half, upper, swap(lower)).astype(BF)
        return carry

    lax.fori_loop(0, count, deal, 0)


def norm_rows(values):
    centered = values - jnp.mean(values, axis=-1, keepdims=True)
    spread_of = jnp.mean(centered * centered, axis=-1, keepdims=True)
    return centered * lax.rsqrt(spread_of + 1e-05)


def slots_of(routes, experts):
    rows = routes.shape[0]
    lane = lax.broadcasted_iota(jnp.int32, (rows, 128), 1)
    hot = [(routes[:, k : k + 1] == lane).astype(F32) for k in range(TOPK)]
    picks = (hot[0] + hot[1]).astype(BF)
    below = lax.broadcasted_iota(jnp.int32, (rows, rows), 1) < lax.broadcasted_iota(
        jnp.int32, (rows, rows), 0
    )
    ranks = dot(below.astype(F32).astype(BF), picks)
    slots = [
        routes[:, k : k + 1] * CAP_PAD
        + jnp.sum(hot[k] * ranks, axis=1, keepdims=True).astype(jnp.int32)
        for k in range(TOPK)
    ]
    places = lax.broadcasted_iota(jnp.int32, (rows, experts * CAP_PAD), 1)
    return hot, [(slot == places).astype(F32).astype(BF) for slot in slots]


def middle_kernel(
    tm,
    dp,
    att_ref,
    proj_ref,
    taps_ref,
    router_ref,
    routes_ref,
    lengths_ref,
    arrived_ref,
    second_ref,
    gates_ref,
    heads,
    first_s,
    normed,
    label,
    outgoing,
    send_a,
    recv_a,
    own_a,
    send_b,
    recv_b,
    own_b,
):
    greet("tm", tm)
    greet("dp", dp)
    rows = routes_ref.shape[0]
    wide = rows + 2 * EDGE
    half = wide // 2
    greeted(tm + dp - 2)
    back = spread("tm", tm, att_ref, heads, send_a, recv_a, own_a)
    place = (
        lax.axis_index("tm") * rows - EDGE + lax.broadcasted_iota(jnp.int32, (wide, 128), 0)
    )
    frames = rows * tm
    mark = jnp.zeros((wide, 128), jnp.int32)
    end = jnp.int32(0)
    for r in range(RECS - 1):
        end = end + lengths_ref[0, r]
        mark = mark + (place >= end).astype(jnp.int32)
    mark = jnp.where(place < 0, -1, jnp.where(place >= frames, RECS, mark))
    label[...] = mark
    for copy in back:
        copy.wait()
    low = low_lanes((half, 128))
    for part in range(2):
        tiles = []
        for pair in range(HEADS // 2):
            a = heads[2 * pair].astype(F32)
            b = heads[2 * pair + 1].astype(F32)
            if part == 0:
                tiles.append(jnp.where(low, a, swap(b)).astype(BF))
            else:
                tiles.append(jnp.where(low, swap(a), b).astype(BF))
        attended = jnp.concatenate(tiles, axis=1)
        first = dot(attended, proj_ref[...])
        first_s[pl.ds(part * half, half), :] = first
        unit = norm_rows(first).astype(BF).astype(F32)
        for column in range(D // 128):
            normed[column, pl.ds(part * half, half), :] = unit[:, column * 128 : column * 128 + 128]

    strip = 256
    group = 32

    def conv_rows(step, carry):
        base = pl.multiple_of(step * group, group)
        own = label[pl.ds(base + EDGE, group), :]
        for column in range(D // strip):
            total = [jnp.zeros((group, 128), F32)] * (strip // 128)
            for tap in range(KERNEL):
                shift = tap + EDGE - HALF
                same = label[pl.ds(base + shift, group), :] == own
                for n in range(strip // 128):
                    lanes = slice(column * strip + 128 * n, column * strip + 128 * n + 128)
                    value = normed[column * (strip // 128) + n, pl.ds(base + shift, group), :]
                    total[n] = total[n] + jnp.where(same, value * taps_ref[tap : tap + 1, lanes], 0.0)
            for n in range(strip // 128):
                lanes = slice(column * strip + 128 * n, column * strip + 128 * n + 128)
                second_ref[pl.ds(base, group), lanes] = first_s[
                    pl.ds(base + EDGE, group), lanes
                ] + total[n] / (1.0 + jnp.exp(-total[n]))
        return carry

    lax.fori_loop(0, rows // group, conv_rows, 0)
    mixed = norm_rows(second_ref[...]).astype(BF)
    logits = dot(mixed, router_ref[...])
    hot, places = slots_of(routes_ref[...], dp)
    powers = jnp.exp(logits)
    chosen = [jnp.sum(hot[k] * powers, axis=1, keepdims=True) for k in range(TOPK)]
    whole = chosen[0] + chosen[1]
    lane = lax.broadcasted_iota(jnp.int32, (rows, 128), 1)
    gates_ref[...] = jnp.where(lane == 0, chosen[0] / whole, chosen[1] / whole)
    both = places[0] + places[1]
    for expert in range(dp):
        cut = both[:, expert * CAP_PAD : (expert + 1) * CAP_PAD]
        outgoing[expert] = dot(cut, mixed, ((0,), (0,))).astype(BF)
    for copy in spread("dp", dp, outgoing, arrived_ref, send_b, recv_b, own_b):
        copy.wait()


def experts_kernel(
    dp,
    arrived_ref,
    in_ref,
    out_w_ref,
    routes_ref,
    second_ref,
    gates_ref,
    out_ref,
    hidden,
    produced,
    returned,
    send_sem,
    recv_sem,
    own_sem,
):
    greet("dp", dp)
    rows = routes_ref.shape[0]
    units = in_ref.shape[0]
    count = dp * CAP_PAD
    piece = 512
    for column in range(units // piece):
        cut = slice(column * piece, (column + 1) * piece)
        tokens = arrived_ref[...].reshape(count, D)
        value = dot(tokens, in_ref[cut, :], ((1,), (1,)))
        hidden[:, cut] = (value / (1.0 + jnp.exp(-value))).astype(BF)
    for column in range(D // piece):
        cut = slice(column * piece, (column + 1) * piece)
        value = dot(hidden[...], out_w_ref[:, cut]).astype(BF)
        produced[:, :, cut] = value.reshape(dp, CAP_PAD, piece)
    greeted(dp - 1)
    copies = spread("dp", dp, produced, returned, send_sem, recv_sem, own_sem)
    _, places = slots_of(routes_ref[...], dp)
    for copy in copies:
        copy.wait()
    for column in range(D // piece):
        cut = slice(column * piece, (column + 1) * piece)
        results = returned[:, :, cut].reshape(count, piece)
        mixture = gates_ref[:, 0:1] * dot(places[0], results)
        mixture = mixture + gates_ref[:, 1:2] * dot(places[1], results)
        out_ref[:, cut] = (second_ref[:, cut] + 0.5 * mixture).astype(BF)


def params(collective_id=None):
    if collective_id is None:
        return pltpu.CompilerParams(vmem_limit_bytes=VMEM_LIMIT)
    return pltpu.CompilerParams(
        vmem_limit_bytes=VMEM_LIMIT, collective_id=collective_id, has_side_effects=True
    )


def exchange_sems(count):
    return [
        pltpu.SemaphoreType.DMA((count - 1,)),
        pltpu.SemaphoreType.DMA((count - 1,)),
        pltpu.SemaphoreType.DMA,
    ]


def body(
    query_rows,
    key_rows,
    value_rows,
    head_scale,
    out_proj,
    conv_taps,
    router,
    expert_in,
    expert_out,
    lengths,
    routes,
):
    rows = query_rows.shape[1]
    tm = lax.axis_size("tm")
    dp = lax.axis_size("dp")
    frames = rows * tm
    wide = rows + 2 * EDGE
    stacked = rows + rows // 2
    piece_in = lax.all_gather(expert_in[0], "tm", axis=0, tiled=True)
    piece_out = lax.all_gather(expert_out[0], "tm", axis=0, tiled=True)
    units = piece_in.shape[0]
    packed = pl.pallas_call(
        functools.partial(heads_kernel, tm),
        out_shape=jax.ShapeDtypeStruct((tm, stacked, 128), BF),
        in_specs=[vmem_spec()] * 3,
        out_specs=any_spec(),
        scratch_shapes=[pltpu.VMEM((tm, stacked, 128), BF)] + exchange_sems(tm),
        compiler_params=params(0),
        name="heads",
    )(query_rows[0], key_rows[0], value_rows[0])
    attended = pl.pallas_call(
        functools.partial(attend_kernel, tm),
        out_shape=jax.ShapeDtypeStruct((tm, wide // 2, 128), BF),
        in_specs=[smem_spec(), smem_spec(), vmem_spec()],
        out_specs=vmem_spec(),
        scratch_shapes=[
            pltpu.VMEM((frames, 128), BF),
            pltpu.VMEM((frames, 128), BF),
            pltpu.VMEM((frames, 128), BF),
            pltpu.VMEM((frames + 2 * EDGE, 128), BF),
            pltpu.VMEM((8, frames), jnp.int32),
            pltpu.VMEM((TQ, 128), jnp.int32),
        ],
        compiler_params=params(),
        name="attend",
    )(head_scale, lengths, packed)
    wide_router = jnp.pad(router, ((0, 0), (0, 128 - router.shape[1])))
    arrived, second, gates = pl.pallas_call(
        functools.partial(middle_kernel, tm, dp),
        out_shape=(
            jax.ShapeDtypeStruct((dp, CAP_PAD, D), BF),
            jax.ShapeDtypeStruct((rows, D), F32),
            jax.ShapeDtypeStruct((rows, 128), F32),
        ),
        in_specs=[any_spec()] + [vmem_spec()] * 4 + [smem_spec()],
        out_specs=(any_spec(), vmem_spec(), vmem_spec()),
        scratch_shapes=[
            pltpu.VMEM((tm, wide // 2, 128), BF),
            pltpu.VMEM((wide, D), F32),
            pltpu.VMEM((D // 128, wide, 128), F32),
            pltpu.VMEM((wide, 128), jnp.int32),
            pltpu.VMEM((dp, CAP_PAD, D), BF),
        ]
        + exchange_sems(tm)
        + exchange_sems(dp),
        compiler_params=params(1),
        name="middle",
    )(attended, out_proj, conv_taps, wide_router, routes[0], lengths)
    out = pl.pallas_call(
        functools.partial(experts_kernel, dp),
        out_shape=jax.ShapeDtypeStruct((rows, D), BF),
        in_specs=[vmem_spec()] * 6,
        out_specs=vmem_spec(),
        scratch_shapes=[
            pltpu.VMEM((dp * CAP_PAD, units), BF),
            pltpu.VMEM((dp, CAP_PAD, D), BF),
            pltpu.VMEM((dp, CAP_PAD, D), BF),
        ]
        + exchange_sems(dp),
        compiler_params=params(2),
        name="experts",
    )(arrived, piece_in, piece_out, routes[0], second, gates)
    return out[None]


def solution(mesh):
    return jax.shard_map(
        body,
        mesh=mesh,
        in_specs=(
            P("dp", "tm", None),
            P("dp", "tm", None),
            P("dp", "tm", None),
            P(),
            P(),
            P(),
            P(),
            P("dp", "tm", None),
            P("dp", "tm", None),
            P("dp", None),
            P("dp", "tm", None),
        ),
        out_specs=P("dp", "tm", None),
        check_vma=False,
    )
```

```python
import functools

import jax
import jax.numpy as jnp
from jax import lax
from jax.experimental import pallas as pl
from jax.experimental.pallas import tpu as pltpu
from jax.sharding import PartitionSpec as P

D = 1536
HEADS = 16
HEAD_DIM = 64
KERNEL = 31
HALF = 15
TOPK = 2
RECS = 4
EDGE = 16
CAP_PAD = 48
MESH = pl.DeviceIdType.MESH
BF = jnp.bfloat16
F32 = jnp.float32
VMEM_LIMIT = 60 * 1024 * 1024


def any_spec():
    return pl.BlockSpec(memory_space=pl.ANY)


def vmem_spec():
    return pl.BlockSpec(memory_space=pltpu.VMEM)


def smem_spec():
    return pl.BlockSpec(memory_space=pltpu.SMEM)


def dot(a, b, dims=((1,), (0,))):
    return lax.dot_general(a, b, (dims, ((), ())), preferred_element_type=F32)


def greet(axis, count):
    barrier = pltpu.get_barrier_semaphore()
    me = lax.axis_index(axis)
    for step in range(1, count):
        pl.semaphore_signal(
            barrier, inc=1, device_id={axis: lax.rem(me + step, count)}, device_id_type=MESH
        )


def greeted(total):
    pl.semaphore_wait(pltpu.get_barrier_semaphore(), total)


def spread(axis, count, source, target, send_sem, recv_sem, own_sem):
    me = lax.axis_index(axis)
    copies = []
    for step in range(1, count):
        peer = lax.rem(me + step, count)
        copy = pltpu.make_async_remote_copy(
            src_ref=source.at[peer],
            dst_ref=target.at[me],
            send_sem=send_sem.at[step - 1],
            recv_sem=recv_sem.at[step - 1],
            device_id={axis: peer},
            device_id_type=MESH,
        )
        copy.start()
        copies.append(copy)
    own = pltpu.make_async_copy(source.at[me], target.at[me], own_sem)
    own.start()
    copies.append(own)
    return copies


def low_lanes(shape):
    return lax.broadcasted_iota(jnp.int32, shape, 1) < HEAD_DIM


def pair_ones():
    row = lax.broadcasted_iota(jnp.int32, (128, 128), 0) // HEAD_DIM
    col = lax.broadcasted_iota(jnp.int32, (128, 128), 1) // HEAD_DIM
    return (row == col).astype(F32).astype(BF)


def unit_pair(tile, ones):
    square = tile * tile
    high = square.astype(BF)
    rest = (square - high.astype(F32)).astype(BF)
    total = dot(high, ones) + dot(rest, ones)
    return tile * lax.rsqrt(total + 1e-06)


def swap(tile):
    return pltpu.roll(tile, HEAD_DIM, 1)


def norm_rows(values):
    centered = values - jnp.mean(values, axis=-1, keepdims=True)
    spread_of = jnp.mean(centered * centered, axis=-1, keepdims=True)
    return centered * lax.rsqrt(spread_of + 1e-05)


def slots_of(routes, experts):
    rows = routes.shape[0]
    lane = lax.broadcasted_iota(jnp.int32, (rows, 128), 1)
    hot = [(routes[:, k : k + 1] == lane).astype(F32) for k in range(TOPK)]
    picks = (hot[0] + hot[1]).astype(BF)
    below = lax.broadcasted_iota(jnp.int32, (rows, rows), 1) < lax.broadcasted_iota(
        jnp.int32, (rows, rows), 0
    )
    ranks = dot(below.astype(F32).astype(BF), picks)
    slots = [
        routes[:, k : k + 1] * CAP_PAD
        + jnp.sum(hot[k] * ranks, axis=1, keepdims=True).astype(jnp.int32)
        for k in range(TOPK)
    ]
    places = lax.broadcasted_iota(jnp.int32, (rows, experts * CAP_PAD), 1)
    return hot, [(slot == places).astype(F32).astype(BF) for slot in slots]


GATHER_IDS = 30
HOPS = 4


class Gather:
    def __init__(self, w_in, w_out, send_sem, recv_sem):
        self.w_in, self.w_out = w_in, w_out
        self.send_sem, self.recv_sem = send_sem, recv_sem
        self.me = lax.axis_index("tm")
        self.own = self.me // 8 * 8
        self.other = 8 - self.own
        self.z = self.me - self.own

    def at(self, base, shift):
        return base + lax.rem(self.z + shift + 8, 8)

    def table(self):
        w_in, w_out, own, other, at = self.w_in, self.w_out, self.own, self.other, self.at
        up, down, across = at(own, 1), at(own, -1), at(other, 0)
        table = {0: (w_in, self.me, across, across), 1: (w_out, self.me, across, across)}
        for h in range(1, HOPS + 1):
            table[1 + h] = (w_out, at(own, -h), across, at(other, -h))
            table[8 + h] = (w_out, at(own, 1 - h), up, at(own, -h))
            table[15 + h] = (w_in, at(own, 1 - h), up, at(own, -h))
            table[25 + h] = (w_in, at(other, h - 1), down, at(other, h))
        for h in range(1, HOPS):
            table[5 + h] = (w_out, at(own, h), across, at(other, h))
            table[12 + h] = (w_out, at(own, h - 1), down, at(own, h))
            table[19 + h] = (w_in, at(other, 1 - h), up, at(other, -h))
            table[22 + h] = (w_in, at(own, h - 1), down, at(own, h))
        return table

    def copy(self, n, chunk):
        buffer, _, peer, _ = self.table()[n]
        return pltpu.make_async_remote_copy(
            src_ref=buffer.at[chunk],
            dst_ref=buffer.at[chunk],
            send_sem=self.send_sem.at[n],
            recv_sem=self.recv_sem.at[n],
            device_id={"tm": peer},
            device_id_type=MESH,
        )

    def start(self, *ids):
        for n in ids:
            self.copy(n, self.table()[n][1]).start()

    def receive(self, *ids):
        for n in ids:
            self.copy(n, self.table()[n][3]).wait_recv()

    def finish(self):
        for n in range(GATHER_IDS):
            self.copy(n, self.table()[n][1]).wait_send()

    def event(self, n):
        if n == 0:
            self.start(0, 1, 9, 13)
        elif n == 1:
            self.receive(0)
            self.start(16, 23, 20, 26)
        elif n == 2:
            self.receive(9, 13)
            self.start(10, 14, 2, 6)
        elif n == 3:
            self.receive(16, 23, 20, 26)
            self.start(17, 24, 21, 27)
        elif n == 4:
            self.receive(10, 14)
            self.start(11, 15, 3, 7)
        elif n == 5:
            self.receive(17, 24, 21, 27)
            self.start(18, 25, 22, 28)
        elif n == 6:
            self.receive(11, 15)
            self.start(12, 4, 8)
        elif n == 7:
            self.receive(18, 25, 22, 28)
            self.start(19, 29)
        elif n == 8:
            self.receive(12)
            self.start(5)
        elif n == 9:
            self.receive(19, 29)
        else:
            self.receive(1, 2, 3, 4, 5, 6, 7, 8)


def block_kernel(
    tm,
    dp,
    scale_ref,
    lengths_ref,
    q_ref,
    k_ref,
    v_ref,
    proj_ref,
    taps_ref,
    router_ref,
    routes_ref,
    in_ref,
    out_w_ref,
    out_ref,
    pack,
    held,
    qs,
    ks,
    vs,
    outs,
    att,
    heads,
    first_s,
    normed,
    label,
    second,
    outgoing,
    arrived,
    w_in,
    w_out,
    hidden,
    produced,
    returned,
    gather_send,
    gather_recv,
    load_sem,
    send_h,
    recv_h,
    own_h,
    send_a,
    recv_a,
    send_b,
    recv_b,
    own_b,
    send_c,
    recv_c,
):
    greet("tm", tm)
    greet("dp", dp)
    me = lax.axis_index("tm")
    me_dp = lax.axis_index("dp")
    rows = q_ref.shape[0]
    frames = rows * tm
    part = rows // 2
    wide = rows + 2 * EDGE
    half = wide // 2
    gather = Gather(w_in, w_out, gather_send, gather_recv)
    loads = [
        pltpu.make_async_copy(in_ref.at[0], w_in.at[me], load_sem.at[0]),
        pltpu.make_async_copy(out_w_ref.at[0], w_out.at[me], load_sem.at[1]),
    ]
    for load in loads:
        load.start()
    for load in loads:
        load.wait()
    greeted(tm + dp - 2)
    gather.event(0)

    ones = pair_ones()
    low = low_lanes((rows, 128))
    low_part = low_lanes((part, 128))
    low_half = low_lanes((half, 128))
    for pair in range(HEADS // 2):
        lanes = slice(128 * pair, 128 * pair + 128)
        q = unit_pair(q_ref[:, lanes].astype(F32), ones)
        k = unit_pair(k_ref[:, lanes].astype(F32), ones)
        pack[2 * pair, :rows, :] = jnp.where(low, q, swap(k)).astype(BF)
        pack[2 * pair + 1, :rows, :] = jnp.where(low, swap(q), k).astype(BF)
        upper = v_ref[:part, lanes].astype(F32)
        lower = v_ref[part:, lanes].astype(F32)
        pack[2 * pair, rows:, :] = jnp.where(low_part, upper, swap(lower)).astype(BF)
        pack[2 * pair + 1, rows:, :] = jnp.where(low_part, swap(upper), lower).astype(BF)
    exchange = spread("tm", tm, pack, held, send_h, recv_h, own_h)
    for copy in exchange:
        copy.wait()
    gather.event(1)

    scale = scale_ref[me] * 1.4426950408889634
    ends = []
    for r in range(RECS - 1):
        ends.append(lengths_ref[0, r] + (ends[-1] if ends else 0))
    lane = lax.broadcasted_iota(jnp.int32, (rows, 128), 1)
    minus = lane == HEAD_DIM + RECS

    def unpack(block, carry):
        base = pl.multiple_of(block * rows, 32)
        tile = held[block, :rows, :].astype(F32)
        spot = base + lax.broadcasted_iota(jnp.int32, (rows, 128), 0)
        mark = sum((spot >= end).astype(jnp.int32) for end in ends)
        hit = lane == HEAD_DIM + mark
        apart = jnp.where(hit | (lane > HEAD_DIM + RECS), 0.0, -128.0)
        qs[pl.ds(base, rows), :] = jnp.where(low, tile, jnp.where(minus, -1.0, apart)).astype(BF)
        ks[pl.ds(base, rows), :] = jnp.where(
            low, swap(tile), jnp.where(minus | hit, 1.0, 0.0)
        ).astype(BF)
        values = held[block, rows:, :].astype(F32)
        vs[pl.ds(base, part), :] = jnp.where(low_part, values, 1.0).astype(BF)
        vs[pl.ds(base + part, part), :] = jnp.where(low_part, swap(values), 1.0).astype(BF)
        return carry

    lax.fori_loop(0, tm, unpack, 0)
    outs[:EDGE, :] = jnp.zeros((EDGE, 128), BF)
    outs[EDGE + frames :, :] = jnp.zeros((EDGE, 128), BF)

    def deal(block):
        base = pl.multiple_of(block * rows, 32)
        upper = outs[pl.ds(base, half), :].astype(F32)
        lower = outs[pl.ds(base + half, half), :].astype(F32)
        return jnp.where(low_half, upper, swap(lower)).astype(BF)

    def back(distance):
        peer = lax.rem(me + distance, tm)
        return pltpu.make_async_remote_copy(
            src_ref=att.at[peer],
            dst_ref=heads.at[me],
            send_sem=send_a.at[distance - 1],
            recv_sem=recv_a.at[distance - 1],
            device_id={"tm": peer},
            device_id_type=MESH,
        )

    def attend(step, carry):
        base = pl.multiple_of(lax.rem(me + 1 + step, tm) * rows, 32)
        scores = dot(qs[pl.ds(base, rows), :], ks[...], ((1,), (1,)))
        total = dot(jnp.exp2(scores * scale).astype(BF), vs[...])
        outs[pl.ds(EDGE + base, rows), :] = (total / swap(total)).astype(BF)

        @pl.when(step >= 2)
        def _():
            peer = lax.rem(me + step, tm)
            att[peer] = deal(peer)
            back(step).start()

        @pl.when(step == 1)
        def _():
            gather.event(2)

        @pl.when(step == 13)
        def _():
            gather.event(3)

        return carry

    lax.fori_loop(0, tm, attend, 0)
    att[lax.rem(me + 1, tm)] = deal(lax.rem(me + 1, tm))
    back(1).start()
    heads[me] = deal(me)
    place = me * rows - EDGE + lax.broadcasted_iota(jnp.int32, (wide, 128), 0)
    mark = sum((place >= end).astype(jnp.int32) for end in ends)
    label[...] = jnp.where(place < 0, -1, jnp.where(place >= frames, RECS, mark))
    for distance in range(1, tm):
        back(distance).wait()
    gather.event(4)

    for top in range(2):
        tiles = []
        for pair in range(HEADS // 2):
            a = heads[2 * pair].astype(F32)
            b = heads[2 * pair + 1].astype(F32)
            if top == 0:
                tiles.append(jnp.where(low_half, a, swap(b)).astype(BF))
            else:
                tiles.append(jnp.where(low_half, swap(a), b).astype(BF))
        first = dot(jnp.concatenate(tiles, axis=1), proj_ref[...])
        first_s[pl.ds(top * half, half), :] = first
        unit = norm_rows(first).astype(BF).astype(F32)
        for column in range(D // 128):
            normed[column, pl.ds(top * half, half), :] = unit[:, column * 128 : column * 128 + 128]

    strip = 256
    group = 32

    def conv_rows(step, carry):
        base = pl.multiple_of(step * group, group)
        own = label[pl.ds(base + EDGE, group), :]
        for column in range(D // strip):
            total = [jnp.zeros((group, 128), F32)] * (strip // 128)
            for tap in range(KERNEL):
                shift = tap + EDGE - HALF
                same = label[pl.ds(base + shift, group), :] == own
                for n in range(strip // 128):
                    lanes = slice(column * strip + 128 * n, column * strip + 128 * n + 128)
                    value = normed[column * (strip // 128) + n, pl.ds(base + shift, group), :]
                    total[n] = total[n] + jnp.where(same, value * taps_ref[tap : tap + 1, lanes], 0.0)
            for n in range(strip // 128):
                lanes = slice(column * strip + 128 * n, column * strip + 128 * n + 128)
                second[pl.ds(base, group), lanes] = first_s[
                    pl.ds(base + EDGE, group), lanes
                ] + total[n] / (1.0 + jnp.exp(-total[n]))

        @pl.when(step == 5)
        def _():
            gather.event(5)

        return carry

    lax.fori_loop(0, rows // group, conv_rows, 0)

    mixed = norm_rows(second[...]).astype(BF)
    logits = dot(mixed, router_ref[...])
    hot, places = slots_of(routes_ref[...], dp)
    powers = jnp.exp(logits)
    chosen = [jnp.sum(hot[k] * powers, axis=1, keepdims=True) for k in range(TOPK)]
    whole = chosen[0] + chosen[1]
    gates = [chosen[k] / whole for k in range(TOPK)]
    both = places[0] + places[1]
    for expert in range(dp):
        cut = both[:, expert * CAP_PAD : (expert + 1) * CAP_PAD]
        outgoing[expert] = dot(cut, mixed, ((0,), (0,))).astype(BF)
    dispatch = spread("dp", dp, outgoing, arrived, send_b, recv_b, own_b)
    for n in range(6, 10):
        gather.event(n)
    for copy in dispatch:
        copy.wait()

    units = w_in.shape[0] * w_in.shape[1]
    chunk = w_in.shape[1]
    count = dp * CAP_PAD
    step_chunks = 4
    for column in range(tm // step_chunks):
        cut = slice(column * step_chunks * chunk, (column + 1) * step_chunks * chunk)
        weights = w_in[column * step_chunks : (column + 1) * step_chunks].reshape(-1, D)
        value = dot(arrived[...].reshape(count, D), weights, ((1,), (1,)))
        hidden[:, cut] = (value / (1.0 + jnp.exp(-value))).astype(BF)
    gather.event(10)
    piece = 512
    team = 4
    results = []
    for turn in range(dp // team):
        base = lax.rem(me_dp // team + 1 + turn, dp // team) * team
        start = pl.multiple_of(base * CAP_PAD, team * CAP_PAD)
        for column in range(D // piece):
            cut = slice(column * piece, (column + 1) * piece)
            weights = w_out[:, :, cut].reshape(units, piece)
            value = dot(hidden[pl.ds(start, team * CAP_PAD), :], weights).astype(BF)
            produced[pl.ds(base, team), :, cut] = value.reshape(team, CAP_PAD, piece)
        for n in range(team):
            if turn == dp // team - 1 and n == 0:
                continue
            peer = base + lax.rem(lax.rem(me_dp, team) + n, team)
            distance = lax.rem(peer - me_dp + dp, dp)
            copy = pltpu.make_async_remote_copy(
                src_ref=produced.at[peer],
                dst_ref=returned.at[me_dp],
                send_sem=send_c.at[distance - 1],
                recv_sem=recv_c.at[distance - 1],
                device_id={"dp": peer},
                device_id_type=MESH,
            )
            copy.start()
            results.append(copy)
    returned[me_dp] = produced[me_dp]
    gather.finish()
    for copy in results:
        copy.wait()
    for column in range(D // piece):
        cut = slice(column * piece, (column + 1) * piece)
        value = returned[:, :, cut].reshape(count, piece)
        mixture = gates[0] * dot(places[0], value) + gates[1] * dot(places[1], value)
        out_ref[:, cut] = (second[:, cut] + 0.5 * mixture).astype(BF)


def sems(count):
    return [pltpu.SemaphoreType.DMA((count,))] * 2


def body(
    query_rows,
    key_rows,
    value_rows,
    head_scale,
    out_proj,
    conv_taps,
    router,
    expert_in,
    expert_out,
    lengths,
    routes,
):
    rows = query_rows.shape[1]
    tm = lax.axis_size("tm")
    dp = lax.axis_size("dp")
    frames = rows * tm
    wide = rows + 2 * EDGE
    stacked = rows + rows // 2
    chunk = expert_in.shape[1]
    wide_router = jnp.pad(router, ((0, 0), (0, 128 - router.shape[1])))
    bf = lambda *shape: pltpu.VMEM(shape, BF)
    out = pl.pallas_call(
        functools.partial(block_kernel, tm, dp),
        out_shape=jax.ShapeDtypeStruct((rows, D), BF),
        in_specs=[smem_spec()] * 2 + [vmem_spec()] * 7 + [any_spec()] * 2,
        out_specs=vmem_spec(),
        scratch_shapes=[
            bf(tm, stacked, 128),
            bf(tm, stacked, 128),
            bf(frames, 128),
            bf(frames, 128),
            bf(frames, 128),
            bf(frames + 2 * EDGE, 128),
            bf(tm, wide // 2, 128),
            bf(tm, wide // 2, 128),
            pltpu.VMEM((wide, D), F32),
            pltpu.VMEM((D // 128, wide, 128), F32),
            pltpu.VMEM((wide, 128), jnp.int32),
            pltpu.VMEM((rows, D), F32),
            bf(dp, CAP_PAD, D),
            bf(dp, CAP_PAD, D),
            bf(tm, chunk, D),
            bf(tm, chunk, D),
            bf(dp * CAP_PAD, tm * chunk),
            bf(dp, CAP_PAD, D),
            bf(dp, CAP_PAD, D),
        ]
        + sems(GATHER_IDS)
        + [pltpu.SemaphoreType.DMA((2,))]
        + sems(tm - 1)
        + [pltpu.SemaphoreType.DMA]
        + sems(tm - 1)
        + sems(dp - 1)
        + [pltpu.SemaphoreType.DMA]
        + sems(dp - 1),
        compiler_params=pltpu.CompilerParams(
            vmem_limit_bytes=VMEM_LIMIT, collective_id=0, has_side_effects=True
        ),
        name="block",
    )(
        head_scale,
        lengths,
        query_rows[0],
        key_rows[0],
        value_rows[0],
        out_proj,
        conv_taps,
        wide_router,
        routes[0],
        expert_in,
        expert_out,
    )
    return out[None]


def solution(mesh):
    return jax.shard_map(
        body,
        mesh=mesh,
        in_specs=(
            P("dp", "tm", None),
            P("dp", "tm", None),
            P("dp", "tm", None),
            P(),
            P(),
            P(),
            P(),
            P("dp", "tm", None),
            P("dp", "tm", None),
            P("dp", None),
            P("dp", "tm", None),
        ),
        out_specs=P("dp", "tm", None),
        check_vma=False,
    )
```

```python
import functools

import jax
import jax.numpy as jnp
from jax import lax
from jax.experimental import pallas as pl
from jax.experimental.pallas import tpu as pltpu
from jax.sharding import PartitionSpec as P

D = 1536
HEADS = 16
HEAD_DIM = 64
KERNEL = 31
HALF = 15
TOPK = 2
RECS = 4
EDGE = 16
CAP_PAD = 48
MESH = pl.DeviceIdType.MESH
BF = jnp.bfloat16
F32 = jnp.float32
VMEM_LIMIT = 60 * 1024 * 1024


def any_spec():
    return pl.BlockSpec(memory_space=pl.ANY)


def vmem_spec():
    return pl.BlockSpec(memory_space=pltpu.VMEM)


def smem_spec():
    return pl.BlockSpec(memory_space=pltpu.SMEM)


def dot(a, b, dims=((1,), (0,))):
    return lax.dot_general(a, b, (dims, ((), ())), preferred_element_type=F32)


def greet(axis, count):
    barrier = pltpu.get_barrier_semaphore()
    me = lax.axis_index(axis)
    for step in range(1, count):
        pl.semaphore_signal(
            barrier, inc=1, device_id={axis: lax.rem(me + step, count)}, device_id_type=MESH
        )


def greeted(total):
    pl.semaphore_wait(pltpu.get_barrier_semaphore(), total)


def spread(axis, count, source, target, send_sem, recv_sem, own_sem):
    me = lax.axis_index(axis)
    copies = []
    for step in range(1, count):
        peer = lax.rem(me + step, count)
        copy = pltpu.make_async_remote_copy(
            src_ref=source.at[peer],
            dst_ref=target.at[me],
            send_sem=send_sem.at[step - 1],
            recv_sem=recv_sem.at[step - 1],
            device_id={axis: peer},
            device_id_type=MESH,
        )
        copy.start()
        copies.append(copy)
    own = pltpu.make_async_copy(source.at[me], target.at[me], own_sem)
    own.start()
    copies.append(own)
    return copies


def low_lanes(shape):
    return lax.broadcasted_iota(jnp.int32, shape, 1) < HEAD_DIM


def pair_ones():
    row = lax.broadcasted_iota(jnp.int32, (128, 128), 0) // HEAD_DIM
    col = lax.broadcasted_iota(jnp.int32, (128, 128), 1) // HEAD_DIM
    return (row == col).astype(F32).astype(BF)


def unit_pair(tile, ones):
    square = tile * tile
    high = square.astype(BF)
    rest = (square - high.astype(F32)).astype(BF)
    total = dot(high, ones) + dot(rest, ones)
    return tile * lax.rsqrt(total + 1e-06)


def swap(tile):
    return pltpu.roll(tile, HEAD_DIM, 1)


def norm_rows(values):
    centered = values - jnp.mean(values, axis=-1, keepdims=True)
    spread_of = jnp.mean(centered * centered, axis=-1, keepdims=True)
    return centered * lax.rsqrt(spread_of + 1e-05)


def slots_of(routes, experts):
    rows = routes.shape[1]
    expert = lax.broadcasted_iota(jnp.int32, (experts, rows), 0)
    hot = [(routes[k : k + 1, :] == expert).astype(F32) for k in range(TOPK)]
    picks = (hot[0] + hot[1]).astype(BF)
    earlier = lax.broadcasted_iota(jnp.int32, (rows, rows), 0) < lax.broadcasted_iota(
        jnp.int32, (rows, rows), 1
    )
    ranks = dot(picks, earlier.astype(F32).astype(BF))
    slots = [
        routes[k : k + 1, :].astype(F32) * CAP_PAD + jnp.sum(hot[k] * ranks, axis=0, keepdims=True)
        for k in range(TOPK)
    ]
    return hot, slots


GATHER_IDS = 30
HOPS = 4


class Gather:
    def __init__(self, w_in, w_out, send_sem, recv_sem):
        self.w_in, self.w_out = w_in, w_out
        self.send_sem, self.recv_sem = send_sem, recv_sem
        self.me = lax.axis_index("tm")
        self.own = self.me // 8 * 8
        self.other = 8 - self.own
        self.z = self.me - self.own

    def at(self, base, shift):
        return base + lax.rem(self.z + shift + 8, 8)

    def table(self):
        w_in, w_out, own, other, at = self.w_in, self.w_out, self.own, self.other, self.at
        up, down, across = at(own, 1), at(own, -1), at(other, 0)
        table = {0: (w_in, self.me, across, across), 1: (w_out, self.me, across, across)}
        for h in range(1, HOPS + 1):
            table[1 + h] = (w_out, at(own, -h), across, at(other, -h))
            table[8 + h] = (w_out, at(own, 1 - h), up, at(own, -h))
            table[15 + h] = (w_in, at(own, 1 - h), up, at(own, -h))
            table[25 + h] = (w_in, at(other, h - 1), down, at(other, h))
        for h in range(1, HOPS):
            table[5 + h] = (w_out, at(own, h), across, at(other, h))
            table[12 + h] = (w_out, at(own, h - 1), down, at(own, h))
            table[19 + h] = (w_in, at(other, 1 - h), up, at(other, -h))
            table[22 + h] = (w_in, at(own, h - 1), down, at(own, h))
        return table

    def copy(self, n, chunk):
        buffer, _, peer, _ = self.table()[n]
        return pltpu.make_async_remote_copy(
            src_ref=buffer.at[chunk],
            dst_ref=buffer.at[chunk],
            send_sem=self.send_sem.at[n],
            recv_sem=self.recv_sem.at[n],
            device_id={"tm": peer},
            device_id_type=MESH,
        )

    def start(self, *ids):
        for n in ids:
            self.copy(n, self.table()[n][1]).start()

    def receive(self, *ids):
        for n in ids:
            self.copy(n, self.table()[n][3]).wait_recv()

    def finish(self):
        for n in range(GATHER_IDS):
            self.copy(n, self.table()[n][1]).wait_send()

    def event(self, n):
        if n == 0:
            self.start(1, 0, 9, 13)
        elif n == 1:
            self.receive(9, 13)
            self.start(10, 14, 2, 6)
        elif n == 2:
            self.start(16, 23)
        elif n == 3:
            self.receive(10, 14)
            self.start(11, 15, 3, 7)
        elif n == 4:
            self.receive(11, 15)
            self.start(12, 4, 8)
            self.receive(0)
            self.start(20, 26)
        elif n == 5:
            self.receive(12)
            self.start(5)
            self.receive(16, 23)
            self.start(17, 24)
        elif n == 6:
            self.receive(20, 26)
            self.start(21, 27)
        elif n == 7:
            self.receive(17, 24)
            self.start(18, 25)
        elif n == 8:
            self.receive(21, 27)
            self.start(22, 28)
        elif n == 9:
            self.receive(18, 25)
            self.start(19)
            self.receive(22, 28)
            self.start(29)
        elif n == 10:
            self.receive(19, 29)
        else:
            self.receive(1, 2, 3, 4, 5, 6, 7, 8)


def block_kernel(
    tm,
    dp,
    scale_ref,
    lengths_ref,
    q_ref,
    k_ref,
    v_ref,
    proj_ref,
    taps_ref,
    router_ref,
    routes_ref,
    in_ref,
    out_w_ref,
    out_ref,
    pack,
    held,
    qs,
    ks,
    vs,
    outs,
    att,
    heads,
    first_s,
    normed,
    label,
    second,
    outgoing,
    arrived,
    w_in,
    w_out,
    hidden,
    produced,
    returned,
    placing,
    picking,
    hots,
    numbers,
    gather_send,
    gather_recv,
    load_sem,
    send_h,
    recv_h,
    own_h,
    send_a,
    recv_a,
    send_b,
    recv_b,
    own_b,
    send_c,
    recv_c,
):
    greet("tm", tm)
    greet("dp", dp)
    me = lax.axis_index("tm")
    me_dp = lax.axis_index("dp")
    rows = q_ref.shape[0]
    frames = rows * tm
    part = rows // 2
    wide = rows + 2 * EDGE
    half = wide // 2
    gather = Gather(w_in, w_out, gather_send, gather_recv)
    loads = [
        pltpu.make_async_copy(in_ref.at[0], w_in.at[me], load_sem.at[0]),
        pltpu.make_async_copy(out_w_ref.at[0], w_out.at[me], load_sem.at[1]),
    ]
    for load in loads:
        load.start()
    for load in loads:
        load.wait()
    greeted(tm + dp - 2)
    gather.event(0)

    ones = pair_ones()
    low = low_lanes((rows, 128))
    low_part = low_lanes((part, 128))
    low_half = low_lanes((half, 128))
    for pair in range(HEADS // 2):
        lanes = slice(128 * pair, 128 * pair + 128)
        q = unit_pair(q_ref[:, lanes].astype(F32), ones)
        k = unit_pair(k_ref[:, lanes].astype(F32), ones)
        pack[2 * pair, :rows, :] = jnp.where(low, q, swap(k)).astype(BF)
        pack[2 * pair + 1, :rows, :] = jnp.where(low, swap(q), k).astype(BF)
        upper = v_ref[:part, lanes].astype(F32)
        lower = v_ref[part:, lanes].astype(F32)
        pack[2 * pair, rows:, :] = jnp.where(low_part, upper, swap(lower)).astype(BF)
        pack[2 * pair + 1, rows:, :] = jnp.where(low_part, swap(upper), lower).astype(BF)
    exchange = spread("tm", tm, pack, held, send_h, recv_h, own_h)
    gather.event(1)
    hot, slots = slots_of(routes_ref[...], dp)
    count = dp * CAP_PAD
    spots = lax.broadcasted_iota(jnp.int32, (count, rows), 0).astype(F32)
    placing[...] = ((slots[0] == spots) | (slots[1] == spots)).astype(F32).astype(BF)
    numbers[...] = jnp.zeros_like(numbers)
    for k in range(TOPK):
        hots[k] = hot[k]
        numbers[k : k + 1, :] = slots[k]
    for copy in exchange:
        copy.wait()
    gather.event(2)

    scale = scale_ref[me] * 1.4426950408889634
    ends = []
    for r in range(RECS - 1):
        ends.append(lengths_ref[0, r] + (ends[-1] if ends else 0))
    lane = lax.broadcasted_iota(jnp.int32, (rows, 128), 1)
    minus = lane == HEAD_DIM + RECS

    def unpack(block, carry):
        base = pl.multiple_of(block * rows, 32)
        tile = held[block, :rows, :].astype(F32)
        spot = base + lax.broadcasted_iota(jnp.int32, (rows, 128), 0)
        mark = sum((spot >= end).astype(jnp.int32) for end in ends)
        hit = lane == HEAD_DIM + mark
        apart = jnp.where(hit | (lane > HEAD_DIM + RECS), 0.0, -128.0)
        qs[pl.ds(base, rows), :] = jnp.where(low, tile, jnp.where(minus, -1.0, apart)).astype(BF)
        ks[pl.ds(base, rows), :] = jnp.where(
            low, swap(tile), jnp.where(minus | hit, 1.0, 0.0)
        ).astype(BF)
        values = held[block, rows:, :].astype(F32)
        vs[pl.ds(base, part), :] = jnp.where(low_part, values, 1.0).astype(BF)
        vs[pl.ds(base + part, part), :] = jnp.where(low_part, swap(values), 1.0).astype(BF)
        return carry

    lax.fori_loop(0, tm, unpack, 0)
    outs[:EDGE, :] = jnp.zeros((EDGE, 128), BF)
    outs[EDGE + frames :, :] = jnp.zeros((EDGE, 128), BF)

    def deal(block):
        base = pl.multiple_of(block * rows, 32)
        upper = outs[pl.ds(base, half), :].astype(F32)
        lower = outs[pl.ds(base + half, half), :].astype(F32)
        return jnp.where(low_half, upper, swap(lower)).astype(BF)

    def back(distance):
        peer = lax.rem(me + distance, tm)
        return pltpu.make_async_remote_copy(
            src_ref=att.at[peer],
            dst_ref=heads.at[me],
            send_sem=send_a.at[distance - 1],
            recv_sem=recv_a.at[distance - 1],
            device_id={"tm": peer},
            device_id_type=MESH,
        )

    def attend(step, carry):
        base = pl.multiple_of(lax.rem(me + 1 + step, tm) * rows, 32)
        scores = dot(qs[pl.ds(base, rows), :], ks[...], ((1,), (1,)))
        total = dot(jnp.exp2(scores * scale).astype(BF), vs[...])
        outs[pl.ds(EDGE + base, rows), :] = (total / swap(total)).astype(BF)

        @pl.when(step >= 2)
        def _():
            peer = lax.rem(me + step, tm)
            att[peer] = deal(peer)
            back(step).start()

        @pl.when(step == 2)
        def _():
            gather.event(3)

        @pl.when(step == 8)
        def _():
            gather.event(4)

        return carry

    lax.fori_loop(0, tm, attend, 0)
    att[lax.rem(me + 1, tm)] = deal(lax.rem(me + 1, tm))
    back(1).start()
    heads[me] = deal(me)
    gather.event(5)
    place = me * rows - EDGE + lax.broadcasted_iota(jnp.int32, (wide, 128), 0)
    mark = sum((place >= end).astype(jnp.int32) for end in ends)
    label[...] = jnp.where(place < 0, -1, jnp.where(place >= frames, RECS, mark))
    for distance in range(1, tm):
        back(distance).wait()
    gather.event(6)

    for top in range(2):
        tiles = []
        for pair in range(HEADS // 2):
            a = heads[2 * pair].astype(F32)
            b = heads[2 * pair + 1].astype(F32)
            if top == 0:
                tiles.append(jnp.where(low_half, a, swap(b)).astype(BF))
            else:
                tiles.append(jnp.where(low_half, swap(a), b).astype(BF))
        first = dot(jnp.concatenate(tiles, axis=1), proj_ref[...])
        first_s[pl.ds(top * half, half), :] = first
        unit = norm_rows(first).astype(BF).astype(F32)
        for column in range(D // 128):
            normed[column, pl.ds(top * half, half), :] = unit[:, column * 128 : column * 128 + 128]

    strip = 256
    group = 32

    def conv_rows(step, carry):
        base = pl.multiple_of(step * group, group)
        own = label[pl.ds(base + EDGE, group), :]
        for column in range(D // strip):
            total = [jnp.zeros((group, 128), F32)] * (strip // 128)
            for tap in range(KERNEL):
                shift = tap + EDGE - HALF
                same = label[pl.ds(base + shift, group), :] == own
                for n in range(strip // 128):
                    lanes = slice(column * strip + 128 * n, column * strip + 128 * n + 128)
                    value = normed[column * (strip // 128) + n, pl.ds(base + shift, group), :]
                    total[n] = total[n] + jnp.where(same, value * taps_ref[tap : tap + 1, lanes], 0.0)
            for n in range(strip // 128):
                lanes = slice(column * strip + 128 * n, column * strip + 128 * n + 128)
                second[pl.ds(base, group), lanes] = first_s[
                    pl.ds(base + EDGE, group), lanes
                ] + total[n] / (1.0 + jnp.exp(-total[n]))

        @pl.when(step == 6)
        def _():
            gather.event(7)

        return carry

    lax.fori_loop(0, rows // group, conv_rows, 0)

    mixed = norm_rows(second[...]).astype(BF)
    powers = jnp.exp(dot(router_ref[...], mixed, ((1,), (1,))))
    chosen = [jnp.sum(hots[k] * powers, axis=0, keepdims=True) for k in range(TOPK)]
    whole = chosen[0] + chosen[1]
    for k in range(TOPK):
        numbers[TOPK + k : TOPK + k + 1, :] = chosen[k] / whole
    for expert in range(dp):
        cut = placing[expert * CAP_PAD : (expert + 1) * CAP_PAD, :]
        outgoing[expert] = dot(cut, mixed).astype(BF)
    dispatch = spread("dp", dp, outgoing, arrived, send_b, recv_b, own_b)
    gather.event(8)
    gather.event(9)
    columns = jnp.transpose(numbers[...])
    spots = lax.broadcasted_iota(jnp.int32, (rows, count), 1).astype(F32)
    for k in range(TOPK):
        picking[k] = (columns[:, k : k + 1] == spots).astype(F32).astype(BF)
    gates = [columns[:, TOPK + k : TOPK + k + 1] for k in range(TOPK)]
    for copy in dispatch:
        copy.wait()
    gather.event(10)

    units = w_in.shape[0] * w_in.shape[1]
    chunk = w_in.shape[1]
    step_chunks = 4
    for column in range(tm // step_chunks):
        cut = slice(column * step_chunks * chunk, (column + 1) * step_chunks * chunk)
        weights = w_in[column * step_chunks : (column + 1) * step_chunks].reshape(-1, D)
        value = dot(arrived[...].reshape(count, D), weights, ((1,), (1,)))
        hidden[:, cut] = (value / (1.0 + jnp.exp(-value))).astype(BF)
    gather.event(11)
    piece = 512
    team = 4
    results = []
    for turn in range(dp // team):
        base = lax.rem(me_dp // team + 1 + turn, dp // team) * team
        start = pl.multiple_of(base * CAP_PAD, team * CAP_PAD)
        for column in range(D // piece):
            cut = slice(column * piece, (column + 1) * piece)
            weights = w_out[:, :, cut].reshape(units, piece)
            value = dot(hidden[pl.ds(start, team * CAP_PAD), :], weights).astype(BF)
            produced[pl.ds(base, team), :, cut] = value.reshape(team, CAP_PAD, piece)
        for n in range(team):
            if turn == dp // team - 1 and n == 0:
                continue
            peer = base + lax.rem(lax.rem(me_dp, team) + n, team)
            distance = lax.rem(peer - me_dp + dp, dp)
            copy = pltpu.make_async_remote_copy(
                src_ref=produced.at[peer],
                dst_ref=returned.at[me_dp],
                send_sem=send_c.at[distance - 1],
                recv_sem=recv_c.at[distance - 1],
                device_id={"dp": peer},
                device_id_type=MESH,
            )
            copy.start()
            results.append(copy)
    returned[me_dp] = produced[me_dp]
    gather.finish()
    for copy in results:
        copy.wait()
    for column in range(D // piece):
        cut = slice(column * piece, (column + 1) * piece)
        value = returned[:, :, cut].reshape(count, piece)
        mixture = gates[0] * dot(picking[0], value) + gates[1] * dot(picking[1], value)
        out_ref[:, cut] = (second[:, cut] + 0.5 * mixture).astype(BF)


def sems(count):
    return [pltpu.SemaphoreType.DMA((count,))] * 2


def body(
    query_rows,
    key_rows,
    value_rows,
    head_scale,
    out_proj,
    conv_taps,
    router,
    expert_in,
    expert_out,
    lengths,
    routes,
):
    rows = query_rows.shape[1]
    tm = lax.axis_size("tm")
    dp = lax.axis_size("dp")
    frames = rows * tm
    wide = rows + 2 * EDGE
    stacked = rows + rows // 2
    chunk = expert_in.shape[1]
    bf = lambda *shape: pltpu.VMEM(shape, BF)
    out = pl.pallas_call(
        functools.partial(block_kernel, tm, dp),
        out_shape=jax.ShapeDtypeStruct((rows, D), BF),
        in_specs=[smem_spec()] * 2 + [vmem_spec()] * 7 + [any_spec()] * 2,
        out_specs=vmem_spec(),
        scratch_shapes=[
            bf(tm, stacked, 128),
            bf(tm, stacked, 128),
            bf(frames, 128),
            bf(frames, 128),
            bf(frames, 128),
            bf(frames + 2 * EDGE, 128),
            bf(tm, wide // 2, 128),
            bf(tm, wide // 2, 128),
            pltpu.VMEM((wide, D), F32),
            pltpu.VMEM((D // 128, wide, 128), F32),
            pltpu.VMEM((wide, 128), jnp.int32),
            pltpu.VMEM((rows, D), F32),
            bf(dp, CAP_PAD, D),
            bf(dp, CAP_PAD, D),
            bf(tm, chunk, D),
            bf(tm, chunk, D),
            bf(dp * CAP_PAD, tm * chunk),
            bf(dp, CAP_PAD, D),
            bf(dp, CAP_PAD, D),
            bf(dp * CAP_PAD, rows),
            bf(TOPK, rows, dp * CAP_PAD),
            pltpu.VMEM((TOPK, dp, rows), F32),
            pltpu.VMEM((8, rows), F32),
        ]
        + sems(GATHER_IDS)
        + [pltpu.SemaphoreType.DMA((2,))]
        + sems(tm - 1)
        + [pltpu.SemaphoreType.DMA]
        + sems(tm - 1)
        + sems(dp - 1)
        + [pltpu.SemaphoreType.DMA]
        + sems(dp - 1),
        compiler_params=pltpu.CompilerParams(
            vmem_limit_bytes=VMEM_LIMIT, collective_id=0, has_side_effects=True
        ),
        name="block",
    )(
        head_scale,
        lengths,
        query_rows[0],
        key_rows[0],
        value_rows[0],
        out_proj,
        conv_taps,
        router.T,
        routes[0].T,
        expert_in,
        expert_out,
    )
    return out[None]


def solution(mesh):
    return jax.shard_map(
        body,
        mesh=mesh,
        in_specs=(
            P("dp", "tm", None),
            P("dp", "tm", None),
            P("dp", "tm", None),
            P(),
            P(),
            P(),
            P(),
            P("dp", "tm", None),
            P("dp", "tm", None),
            P("dp", None),
            P("dp", "tm", None),
        ),
        out_specs=P("dp", "tm", None),
        check_vma=False,
    )
```

```python
import functools

import jax
import jax.numpy as jnp
from jax import lax
from jax.experimental import pallas as pl
from jax.experimental.pallas import tpu as pltpu
from jax.sharding import PartitionSpec as P

D = 1536
HEADS = 16
HEAD_DIM = 64
KERNEL = 31
HALF = 15
TOPK = 2
RECS = 4
EDGE = 16
CAP_PAD = 48
MESH = pl.DeviceIdType.MESH
BF = jnp.bfloat16
F32 = jnp.float32
VMEM_LIMIT = 60 * 1024 * 1024


def any_spec():
    return pl.BlockSpec(memory_space=pl.ANY)


def vmem_spec():
    return pl.BlockSpec(memory_space=pltpu.VMEM)


def smem_spec():
    return pl.BlockSpec(memory_space=pltpu.SMEM)


def dot(a, b, dims=((1,), (0,))):
    return lax.dot_general(a, b, (dims, ((), ())), preferred_element_type=F32)


def greet(axis, count):
    barrier = pltpu.get_barrier_semaphore()
    me = lax.axis_index(axis)
    for step in range(1, count):
        pl.semaphore_signal(
            barrier, inc=1, device_id={axis: lax.rem(me + step, count)}, device_id_type=MESH
        )


def greeted(total):
    pl.semaphore_wait(pltpu.get_barrier_semaphore(), total)


def spread(axis, count, source, target, send_sem, recv_sem, own_sem):
    me = lax.axis_index(axis)
    copies = []
    for step in range(1, count):
        peer = lax.rem(me + step, count)
        copy = pltpu.make_async_remote_copy(
            src_ref=source.at[peer],
            dst_ref=target.at[me],
            send_sem=send_sem.at[step - 1],
            recv_sem=recv_sem.at[step - 1],
            device_id={axis: peer},
            device_id_type=MESH,
        )
        copy.start()
        copies.append(copy)
    own = pltpu.make_async_copy(source.at[me], target.at[me], own_sem)
    own.start()
    copies.append(own)
    return copies


def low_lanes(shape):
    return lax.broadcasted_iota(jnp.int32, shape, 1) < HEAD_DIM


def pair_ones():
    row = lax.broadcasted_iota(jnp.int32, (128, 128), 0) // HEAD_DIM
    col = lax.broadcasted_iota(jnp.int32, (128, 128), 1) // HEAD_DIM
    return (row == col).astype(F32).astype(BF)


def unit_pair(tile, ones):
    square = tile * tile
    high = square.astype(BF)
    rest = (square - high.astype(F32)).astype(BF)
    total = dot(high, ones) + dot(rest, ones)
    return tile * lax.rsqrt(total + 1e-06)


def swap(tile):
    return pltpu.roll(tile, HEAD_DIM, 1)


def norm_rows(values):
    centered = values - jnp.mean(values, axis=-1, keepdims=True)
    spread_of = jnp.mean(centered * centered, axis=-1, keepdims=True)
    return centered * lax.rsqrt(spread_of + 1e-05)


def slots_of(routes, experts):
    rows = routes.shape[1]
    expert = lax.broadcasted_iota(jnp.int32, (experts, rows), 0)
    hot = [(routes[k : k + 1, :] == expert).astype(F32) for k in range(TOPK)]
    picks = (hot[0] + hot[1]).astype(BF)
    earlier = lax.broadcasted_iota(jnp.int32, (rows, rows), 0) < lax.broadcasted_iota(
        jnp.int32, (rows, rows), 1
    )
    ranks = dot(picks, earlier.astype(F32).astype(BF))
    slots = [
        routes[k : k + 1, :].astype(F32) * CAP_PAD + jnp.sum(hot[k] * ranks, axis=0, keepdims=True)
        for k in range(TOPK)
    ]
    return hot, slots


GATHER_IDS = 30
HOPS = 4


class Gather:
    def __init__(self, w_in, w_out, send_sem, recv_sem):
        self.w_in, self.w_out = w_in, w_out
        self.send_sem, self.recv_sem = send_sem, recv_sem
        self.me = lax.axis_index("tm")
        self.own = self.me // 8 * 8
        self.other = 8 - self.own
        self.z = self.me - self.own

    def at(self, base, shift):
        return base + lax.rem(self.z + shift + 8, 8)

    def table(self):
        w_in, w_out, own, other, at = self.w_in, self.w_out, self.own, self.other, self.at
        up, down, across = at(own, 1), at(own, -1), at(other, 0)
        table = {0: (w_in, self.me, across, across), 1: (w_out, self.me, across, across)}
        for h in range(1, HOPS + 1):
            table[1 + h] = (w_out, at(own, -h), across, at(other, -h))
            table[8 + h] = (w_out, at(own, 1 - h), up, at(own, -h))
            table[15 + h] = (w_in, at(own, 1 - h), up, at(own, -h))
            table[25 + h] = (w_in, at(other, h - 1), down, at(other, h))
        for h in range(1, HOPS):
            table[5 + h] = (w_out, at(own, h), across, at(other, h))
            table[12 + h] = (w_out, at(own, h - 1), down, at(own, h))
            table[19 + h] = (w_in, at(other, 1 - h), up, at(other, -h))
            table[22 + h] = (w_in, at(own, h - 1), down, at(own, h))
        return table

    def copy(self, n, chunk):
        buffer, _, peer, _ = self.table()[n]
        return pltpu.make_async_remote_copy(
            src_ref=buffer.at[chunk],
            dst_ref=buffer.at[chunk],
            send_sem=self.send_sem.at[n],
            recv_sem=self.recv_sem.at[n],
            device_id={"tm": peer},
            device_id_type=MESH,
        )

    def start(self, *ids):
        for n in ids:
            self.copy(n, self.table()[n][1]).start()

    def receive(self, *ids):
        for n in ids:
            self.copy(n, self.table()[n][3]).wait_recv()

    def finish(self):
        for n in range(GATHER_IDS):
            self.copy(n, self.table()[n][1]).wait_send()

    def event(self, n):
        if n == 0:
            self.start(1, 0, 9, 13)
        elif n == 1:
            self.receive(9, 13)
            self.start(10, 14, 2, 6)
        elif n == 2:
            self.receive(10, 14)
            self.start(11, 15, 3, 7, 16, 23)
        elif n == 3:
            self.receive(11, 15)
            self.start(12, 4, 8)
        elif n == 4:
            self.receive(0)
            self.start(20, 26)
            self.receive(12)
            self.start(5)
            self.receive(16, 23)
            self.start(17, 24)
        elif n == 5:
            self.receive(20, 26)
            self.start(21, 27)
        elif n == 6:
            self.receive(17, 24)
            self.start(18, 25)
            self.receive(21, 27)
            self.start(22, 28)
            self.receive(18, 25)
            self.start(19)
            self.receive(22, 28)
            self.start(29)
        elif n == 7:
            self.receive(19, 29)
        else:
            self.receive(1, 2, 3, 4, 5, 6, 7, 8)


def block_kernel(
    tm,
    dp,
    scale_ref,
    lengths_ref,
    q_ref,
    k_ref,
    v_ref,
    proj_ref,
    taps_ref,
    router_ref,
    routes_ref,
    in_ref,
    out_w_ref,
    out_ref,
    pack,
    held,
    qs,
    ks,
    vs,
    outs,
    att,
    heads,
    first_s,
    normed,
    label,
    second,
    outgoing,
    arrived,
    w_in,
    w_out,
    hidden,
    produced,
    returned,
    placing,
    picking,
    hots,
    numbers,
    gather_send,
    gather_recv,
    load_sem,
    send_h,
    recv_h,
    own_h,
    send_a,
    recv_a,
    send_b,
    recv_b,
    own_b,
    send_c,
    recv_c,
):
    greet("tm", tm)
    greet("dp", dp)
    me = lax.axis_index("tm")
    me_dp = lax.axis_index("dp")
    rows = q_ref.shape[0]
    frames = rows * tm
    part = rows // 2
    wide = rows + 2 * EDGE
    half = wide // 2
    gather = Gather(w_in, w_out, gather_send, gather_recv)
    loads = [
        pltpu.make_async_copy(in_ref.at[0], w_in.at[me], load_sem.at[0]),
        pltpu.make_async_copy(out_w_ref.at[0], w_out.at[me], load_sem.at[1]),
    ]
    for load in loads:
        load.start()
    for load in loads:
        load.wait()
    greeted(tm + dp - 2)
    gather.event(0)

    ones = pair_ones()
    low = low_lanes((rows, 128))
    low_part = low_lanes((part, 128))
    low_half = low_lanes((half, 128))
    for pair in range(HEADS // 2):
        lanes = slice(128 * pair, 128 * pair + 128)
        q = unit_pair(q_ref[:, lanes].astype(F32), ones)
        k = unit_pair(k_ref[:, lanes].astype(F32), ones)
        pack[2 * pair, :rows, :] = jnp.where(low, q, swap(k)).astype(BF)
        pack[2 * pair + 1, :rows, :] = jnp.where(low, swap(q), k).astype(BF)
        upper = v_ref[:part, lanes].astype(F32)
        lower = v_ref[part:, lanes].astype(F32)
        pack[2 * pair, rows:, :] = jnp.where(low_part, upper, swap(lower)).astype(BF)
        pack[2 * pair + 1, rows:, :] = jnp.where(low_part, swap(upper), lower).astype(BF)
    exchange = spread("tm", tm, pack, held, send_h, recv_h, own_h)
    hot, slots = slots_of(routes_ref[...], dp)
    count = dp * CAP_PAD
    spots = lax.broadcasted_iota(jnp.int32, (count, rows), 0).astype(F32)
    placing[...] = ((slots[0] == spots) | (slots[1] == spots)).astype(F32).astype(BF)
    numbers[...] = jnp.zeros_like(numbers)
    for k in range(TOPK):
        hots[k] = hot[k]
        numbers[k : k + 1, :] = slots[k]
    for copy in exchange:
        copy.wait()
    gather.event(1)

    scale = scale_ref[me] * 1.4426950408889634
    ends = []
    for r in range(RECS - 1):
        ends.append(lengths_ref[0, r] + (ends[-1] if ends else 0))
    lane = lax.broadcasted_iota(jnp.int32, (rows, 128), 1)
    minus = lane == HEAD_DIM + RECS

    def unpack(block, carry):
        base = pl.multiple_of(block * rows, 32)
        tile = held[block, :rows, :].astype(F32)
        spot = base + lax.broadcasted_iota(jnp.int32, (rows, 128), 0)
        mark = sum((spot >= end).astype(jnp.int32) for end in ends)
        hit = lane == HEAD_DIM + mark
        apart = jnp.where(hit | (lane > HEAD_DIM + RECS), 0.0, -128.0)
        qs[pl.ds(base, rows), :] = jnp.where(low, tile, jnp.where(minus, -1.0, apart)).astype(BF)
        ks[pl.ds(base, rows), :] = jnp.where(
            low, swap(tile), jnp.where(minus | hit, 1.0, 0.0)
        ).astype(BF)
        values = held[block, rows:, :].astype(F32)
        vs[pl.ds(base, part), :] = jnp.where(low_part, values, 1.0).astype(BF)
        vs[pl.ds(base + part, part), :] = jnp.where(low_part, swap(values), 1.0).astype(BF)
        return carry

    lax.fori_loop(0, tm, unpack, 0)
    outs[:EDGE, :] = jnp.zeros((EDGE, 128), BF)
    outs[EDGE + frames :, :] = jnp.zeros((EDGE, 128), BF)

    def deal(block):
        base = pl.multiple_of(block * rows, 32)
        upper = outs[pl.ds(base, half), :].astype(F32)
        lower = outs[pl.ds(base + half, half), :].astype(F32)
        return jnp.where(low_half, upper, swap(lower)).astype(BF)

    def back(distance):
        peer = lax.rem(me + distance, tm)
        return pltpu.make_async_remote_copy(
            src_ref=att.at[peer],
            dst_ref=heads.at[me],
            send_sem=send_a.at[distance - 1],
            recv_sem=recv_a.at[distance - 1],
            device_id={"tm": peer},
            device_id_type=MESH,
        )

    def attend(step, carry):
        base = pl.multiple_of(lax.rem(me + 1 + step, tm) * rows, 32)
        scores = dot(qs[pl.ds(base, rows), :], ks[...], ((1,), (1,)))
        total = dot(jnp.exp2(scores * scale).astype(BF), vs[...])
        outs[pl.ds(EDGE + base, rows), :] = (total / swap(total)).astype(BF)

        @pl.when(step >= 2)
        def _():
            peer = lax.rem(me + step, tm)
            att[peer] = deal(peer)
            back(step).start()

        @pl.when(step == 5)
        def _():
            gather.event(2)

        @pl.when(step == 12)
        def _():
            gather.event(3)

        return carry

    lax.fori_loop(0, tm, attend, 0)
    att[lax.rem(me + 1, tm)] = deal(lax.rem(me + 1, tm))
    back(1).start()
    heads[me] = deal(me)
    place = me * rows - EDGE + lax.broadcasted_iota(jnp.int32, (wide, 128), 0)
    mark = sum((place >= end).astype(jnp.int32) for end in ends)
    label[...] = jnp.where(place < 0, -1, jnp.where(place >= frames, RECS, mark))
    for distance in range(1, tm):
        back(distance).wait()
    gather.event(4)

    for top in range(2):
        tiles = []
        for pair in range(HEADS // 2):
            a = heads[2 * pair].astype(F32)
            b = heads[2 * pair + 1].astype(F32)
            if top == 0:
                tiles.append(jnp.where(low_half, a, swap(b)).astype(BF))
            else:
                tiles.append(jnp.where(low_half, swap(a), b).astype(BF))
        first = dot(jnp.concatenate(tiles, axis=1), proj_ref[...])
        first_s[pl.ds(top * half, half), :] = first
        unit = norm_rows(first).astype(BF).astype(F32)
        for column in range(D // 128):
            normed[column, pl.ds(top * half, half), :] = unit[:, column * 128 : column * 128 + 128]

    strip = 256
    group = 32

    def conv_rows(step, carry):
        base = pl.multiple_of(step * group, group)
        own = label[pl.ds(base + EDGE, group), :]
        for column in range(D // strip):
            total = [jnp.zeros((group, 128), F32)] * (strip // 128)
            for tap in range(KERNEL):
                shift = tap + EDGE - HALF
                same = label[pl.ds(base + shift, group), :] == own
                for n in range(strip // 128):
                    lanes = slice(column * strip + 128 * n, column * strip + 128 * n + 128)
                    value = normed[column * (strip // 128) + n, pl.ds(base + shift, group), :]
                    total[n] = total[n] + jnp.where(same, value * taps_ref[tap : tap + 1, lanes], 0.0)
            for n in range(strip // 128):
                lanes = slice(column * strip + 128 * n, column * strip + 128 * n + 128)
                second[pl.ds(base, group), lanes] = first_s[
                    pl.ds(base + EDGE, group), lanes
                ] + total[n] / (1.0 + jnp.exp(-total[n]))

        @pl.when(step == 3)
        def _():
            gather.event(5)

        return carry

    lax.fori_loop(0, rows // group, conv_rows, 0)

    mixed = norm_rows(second[...]).astype(BF)
    powers = jnp.exp(dot(router_ref[...], mixed, ((1,), (1,))))
    chosen = [jnp.sum(hots[k] * powers, axis=0, keepdims=True) for k in range(TOPK)]
    whole = chosen[0] + chosen[1]
    for k in range(TOPK):
        numbers[TOPK + k : TOPK + k + 1, :] = chosen[k] / whole
    for expert in range(dp):
        cut = placing[expert * CAP_PAD : (expert + 1) * CAP_PAD, :]
        outgoing[expert] = dot(cut, mixed).astype(BF)
    dispatch = spread("dp", dp, outgoing, arrived, send_b, recv_b, own_b)
    gather.event(6)
    columns = jnp.transpose(numbers[...])
    spots = lax.broadcasted_iota(jnp.int32, (rows, count), 1).astype(F32)
    for k in range(TOPK):
        picking[k] = (columns[:, k : k + 1] == spots).astype(F32).astype(BF)
    gates = [columns[:, TOPK + k : TOPK + k + 1] for k in range(TOPK)]
    for copy in dispatch:
        copy.wait()

    units = w_in.shape[0] * w_in.shape[1]
    chunk = w_in.shape[1]
    for shift in (0, 1, -1, 2, -2, 3, -3, 4):
        if shift == 4:
            gather.event(7)
        pair = [gather.at(gather.own, shift), gather.at(gather.other, shift)]
        weights = jnp.concatenate([w_in[one] for one in pair], axis=0)
        value = dot(arrived[...].reshape(count, D), weights, ((1,), (1,)))
        value = (value / (1.0 + jnp.exp(-value))).astype(BF)
        for n, one in enumerate(pair):
            lanes = pl.ds(pl.multiple_of(one * chunk, chunk), chunk)
            hidden[:, lanes] = value[:, n * chunk : (n + 1) * chunk]
    gather.event(8)
    piece = 512
    team = 4
    results = []
    for turn in range(dp // team):
        base = lax.rem(me_dp // team + 1 + turn, dp // team) * team
        start = pl.multiple_of(base * CAP_PAD, team * CAP_PAD)
        for column in range(D // piece):
            cut = slice(column * piece, (column + 1) * piece)
            weights = w_out[:, :, cut].reshape(units, piece)
            value = dot(hidden[pl.ds(start, team * CAP_PAD), :], weights).astype(BF)
            produced[pl.ds(base, team), :, cut] = value.reshape(team, CAP_PAD, piece)
        for n in range(team):
            if turn == dp // team - 1 and n == 0:
                continue
            peer = base + lax.rem(lax.rem(me_dp, team) + n, team)
            distance = lax.rem(peer - me_dp + dp, dp)
            copy = pltpu.make_async_remote_copy(
                src_ref=produced.at[peer],
                dst_ref=returned.at[me_dp],
                send_sem=send_c.at[distance - 1],
                recv_sem=recv_c.at[distance - 1],
                device_id={"dp": peer},
                device_id_type=MESH,
            )
            copy.start()
            results.append(copy)
    returned[me_dp] = produced[me_dp]
    gather.finish()
    for copy in results:
        copy.wait()
    for column in range(D // piece):
        cut = slice(column * piece, (column + 1) * piece)
        value = returned[:, :, cut].reshape(count, piece)
        mixture = gates[0] * dot(picking[0], value) + gates[1] * dot(picking[1], value)
        out_ref[:, cut] = (second[:, cut] + 0.5 * mixture).astype(BF)


def sems(count):
    return [pltpu.SemaphoreType.DMA((count,))] * 2


def body(
    query_rows,
    key_rows,
    value_rows,
    head_scale,
    out_proj,
    conv_taps,
    router,
    expert_in,
    expert_out,
    lengths,
    routes,
):
    rows = query_rows.shape[1]
    tm = lax.axis_size("tm")
    dp = lax.axis_size("dp")
    frames = rows * tm
    wide = rows + 2 * EDGE
    stacked = rows + rows // 2
    chunk = expert_in.shape[1]
    bf = lambda *shape: pltpu.VMEM(shape, BF)
    out = pl.pallas_call(
        functools.partial(block_kernel, tm, dp),
        out_shape=jax.ShapeDtypeStruct((rows, D), BF),
        in_specs=[smem_spec()] * 2 + [vmem_spec()] * 7 + [any_spec()] * 2,
        out_specs=vmem_spec(),
        scratch_shapes=[
            bf(tm, stacked, 128),
            bf(tm, stacked, 128),
            bf(frames, 128),
            bf(frames, 128),
            bf(frames, 128),
            bf(frames + 2 * EDGE, 128),
            bf(tm, wide // 2, 128),
            bf(tm, wide // 2, 128),
            pltpu.VMEM((wide, D), F32),
            pltpu.VMEM((D // 128, wide, 128), F32),
            pltpu.VMEM((wide, 128), jnp.int32),
            pltpu.VMEM((rows, D), F32),
            bf(dp, CAP_PAD, D),
            bf(dp, CAP_PAD, D),
            bf(tm, chunk, D),
            bf(tm, chunk, D),
            bf(dp * CAP_PAD, tm * chunk),
            bf(dp, CAP_PAD, D),
            bf(dp, CAP_PAD, D),
            bf(dp * CAP_PAD, rows),
            bf(TOPK, rows, dp * CAP_PAD),
            pltpu.VMEM((TOPK, dp, rows), F32),
            pltpu.VMEM((8, rows), F32),
        ]
        + sems(GATHER_IDS)
        + [pltpu.SemaphoreType.DMA((2,))]
        + sems(tm - 1)
        + [pltpu.SemaphoreType.DMA]
        + sems(tm - 1)
        + sems(dp - 1)
        + [pltpu.SemaphoreType.DMA]
        + sems(dp - 1),
        compiler_params=pltpu.CompilerParams(
            vmem_limit_bytes=VMEM_LIMIT, collective_id=0, has_side_effects=True
        ),
        name="block",
    )(
        head_scale,
        lengths,
        query_rows[0],
        key_rows[0],
        value_rows[0],
        out_proj,
        conv_taps,
        router.T,
        routes[0].T,
        expert_in,
        expert_out,
    )
    return out[None]


def solution(mesh):
    return jax.shard_map(
        body,
        mesh=mesh,
        in_specs=(
            P("dp", "tm", None),
            P("dp", "tm", None),
            P("dp", "tm", None),
            P(),
            P(),
            P(),
            P(),
            P("dp", "tm", None),
            P("dp", "tm", None),
            P("dp", None),
            P("dp", "tm", None),
        ),
        out_specs=P("dp", "tm", None),
        check_vma=False,
    )
```

```python
import functools

import jax
import jax.numpy as jnp
from jax import lax
from jax.experimental import pallas as pl
from jax.experimental.pallas import tpu as pltpu
from jax.sharding import PartitionSpec as P

D = 1536
HEADS = 16
HEAD_DIM = 64
KERNEL = 31
HALF = 15
TOPK = 2
RECS = 4
EDGE = 16
CAP_PAD = 48
MESH = pl.DeviceIdType.MESH
BF = jnp.bfloat16
F32 = jnp.float32
VMEM_LIMIT = 60 * 1024 * 1024


def any_spec():
    return pl.BlockSpec(memory_space=pl.ANY)


def vmem_spec():
    return pl.BlockSpec(memory_space=pltpu.VMEM)


def smem_spec():
    return pl.BlockSpec(memory_space=pltpu.SMEM)


def dot(a, b, dims=((1,), (0,))):
    return lax.dot_general(a, b, (dims, ((), ())), preferred_element_type=F32)


def greet(axis, count):
    barrier = pltpu.get_barrier_semaphore()
    me = lax.axis_index(axis)
    for step in range(1, count):
        pl.semaphore_signal(
            barrier, inc=1, device_id={axis: lax.rem(me + step, count)}, device_id_type=MESH
        )


def greeted(total):
    pl.semaphore_wait(pltpu.get_barrier_semaphore(), total)


def spread(axis, count, source, target, send_sem, recv_sem, own_sem):
    me = lax.axis_index(axis)
    copies = []
    for step in range(1, count):
        peer = lax.rem(me + step, count)
        copy = pltpu.make_async_remote_copy(
            src_ref=source.at[peer],
            dst_ref=target.at[me],
            send_sem=send_sem.at[step - 1],
            recv_sem=recv_sem.at[step - 1],
            device_id={axis: peer},
            device_id_type=MESH,
        )
        copy.start()
        copies.append(copy)
    own = pltpu.make_async_copy(source.at[me], target.at[me], own_sem)
    own.start()
    copies.append(own)
    return copies


def low_lanes(shape):
    return lax.broadcasted_iota(jnp.int32, shape, 1) < HEAD_DIM


def pair_ones():
    row = lax.broadcasted_iota(jnp.int32, (128, 128), 0) // HEAD_DIM
    col = lax.broadcasted_iota(jnp.int32, (128, 128), 1) // HEAD_DIM
    return (row == col).astype(F32).astype(BF)


def unit_pair(tile, ones):
    square = tile * tile
    high = square.astype(BF)
    rest = (square - high.astype(F32)).astype(BF)
    total = dot(high, ones) + dot(rest, ones)
    return tile * lax.rsqrt(total + 1e-06)


def swap(tile):
    return pltpu.roll(tile, HEAD_DIM, 1)


def norm_rows(values):
    centered = values - jnp.mean(values, axis=-1, keepdims=True)
    spread_of = jnp.mean(centered * centered, axis=-1, keepdims=True)
    return centered * lax.rsqrt(spread_of + 1e-05)


def slots_of(routes, experts):
    rows = routes.shape[1]
    expert = lax.broadcasted_iota(jnp.int32, (experts, rows), 0)
    hot = [(routes[k : k + 1, :] == expert).astype(F32) for k in range(TOPK)]
    picks = (hot[0] + hot[1]).astype(BF)
    earlier = lax.broadcasted_iota(jnp.int32, (rows, rows), 0) < lax.broadcasted_iota(
        jnp.int32, (rows, rows), 1
    )
    ranks = dot(picks, earlier.astype(F32).astype(BF))
    slots = [
        routes[k : k + 1, :].astype(F32) * CAP_PAD + jnp.sum(hot[k] * ranks, axis=0, keepdims=True)
        for k in range(TOPK)
    ]
    return hot, slots


GATHER_IDS = 30
HOPS = 4


class Gather:
    def __init__(self, w_in, w_out, send_sem, recv_sem):
        self.w_in, self.w_out = w_in, w_out
        self.send_sem, self.recv_sem = send_sem, recv_sem
        self.me = lax.axis_index("tm")
        self.own = self.me // 8 * 8
        self.other = 8 - self.own
        self.z = self.me - self.own

    def at(self, base, shift):
        return base + lax.rem(self.z + shift + 8, 8)

    def table(self):
        w_in, w_out, own, other, at = self.w_in, self.w_out, self.own, self.other, self.at
        up, down, across = at(own, 1), at(own, -1), at(other, 0)
        table = {0: (w_in, self.me, across, across), 1: (w_out, self.me, across, across)}
        for h in range(1, HOPS + 1):
            table[1 + h] = (w_out, at(own, -h), across, at(other, -h))
            table[8 + h] = (w_out, at(own, 1 - h), up, at(own, -h))
            table[15 + h] = (w_in, at(own, 1 - h), up, at(own, -h))
            table[25 + h] = (w_in, at(other, h - 1), down, at(other, h))
        for h in range(1, HOPS):
            table[5 + h] = (w_out, at(own, h), across, at(other, h))
            table[12 + h] = (w_out, at(own, h - 1), down, at(own, h))
            table[19 + h] = (w_in, at(other, 1 - h), up, at(other, -h))
            table[22 + h] = (w_in, at(own, h - 1), down, at(own, h))
        return table

    def copy(self, n, chunk):
        buffer, _, peer, _ = self.table()[n]
        return pltpu.make_async_remote_copy(
            src_ref=buffer.at[chunk],
            dst_ref=buffer.at[chunk],
            send_sem=self.send_sem.at[n],
            recv_sem=self.recv_sem.at[n],
            device_id={"tm": peer},
            device_id_type=MESH,
        )

    def start(self, *ids):
        for n in ids:
            self.copy(n, self.table()[n][1]).start()

    def receive(self, *ids):
        for n in ids:
            self.copy(n, self.table()[n][3]).wait_recv()

    def finish(self):
        for n in range(GATHER_IDS):
            self.copy(n, self.table()[n][1]).wait_send()

    def event(self, n):
        if n == 0:
            self.start(1, 0, 9, 13)
        elif n == 1:
            self.receive(9, 13)
            self.start(10, 14, 2, 6, 16, 23)
        elif n == 2:
            self.receive(10, 14)
            self.start(11, 15, 3, 7)
            self.receive(0)
            self.start(20, 26)
            self.receive(16, 23)
            self.start(17, 24)
        elif n == 3:
            self.receive(20, 26)
            self.start(21, 27)
        elif n == 4:
            self.receive(11, 15)
            self.start(12, 4, 8)
            self.receive(17, 24)
            self.start(18, 25)
            self.receive(21, 27)
            self.start(22, 28)
            self.receive(12)
            self.start(5)
            self.receive(18, 25)
            self.start(19)
            self.receive(22, 28)
            self.start(29)
        elif n == 5:
            self.receive(19, 29)
        else:
            self.receive(1, 2, 3, 4, 5, 6, 7, 8)


def block_kernel(
    tm,
    dp,
    scale_ref,
    lengths_ref,
    q_ref,
    k_ref,
    v_ref,
    proj_hbm,
    taps_hbm,
    router_ref,
    routes_ref,
    in_ref,
    out_w_ref,
    out_ref,
    pack,
    held,
    qs,
    ks,
    vs,
    outs,
    att,
    heads,
    first_s,
    normed,
    label,
    second,
    outgoing,
    arrived,
    w_in,
    w_out,
    hidden,
    produced,
    returned,
    placing,
    picking,
    hots,
    numbers,
    proj_ref,
    taps_ref,
    gather_send,
    gather_recv,
    load_sem,
    send_h,
    recv_h,
    own_h,
    send_a,
    recv_a,
    send_b,
    recv_b,
    own_b,
    send_c,
    recv_c,
):
    greet("tm", tm)
    greet("dp", dp)
    me = lax.axis_index("tm")
    me_dp = lax.axis_index("dp")
    rows = q_ref.shape[0]
    frames = rows * tm
    part = rows // 2
    wide = rows + 2 * EDGE
    half = wide // 2
    gather = Gather(w_in, w_out, gather_send, gather_recv)
    loads = [
        pltpu.make_async_copy(in_ref.at[0], w_in.at[me], load_sem.at[0]),
        pltpu.make_async_copy(out_w_ref.at[0], w_out.at[me], load_sem.at[1]),
    ]
    later = [
        pltpu.make_async_copy(proj_hbm, proj_ref, load_sem.at[2]),
        pltpu.make_async_copy(taps_hbm, taps_ref, load_sem.at[3]),
    ]
    for load in loads + later:
        load.start()
    for load in loads:
        load.wait()
    greeted(tm + dp - 2)
    gather.event(0)

    ones = pair_ones()
    low = low_lanes((rows, 128))
    low_part = low_lanes((part, 128))
    low_half = low_lanes((half, 128))
    for pair in range(HEADS // 2):
        lanes = slice(128 * pair, 128 * pair + 128)
        q = unit_pair(q_ref[:, lanes].astype(F32), ones)
        k = unit_pair(k_ref[:, lanes].astype(F32), ones)
        pack[2 * pair, :rows, :] = jnp.where(low, q, swap(k)).astype(BF)
        pack[2 * pair + 1, :rows, :] = jnp.where(low, swap(q), k).astype(BF)
        upper = v_ref[:part, lanes].astype(F32)
        lower = v_ref[part:, lanes].astype(F32)
        pack[2 * pair, rows:, :] = jnp.where(low_part, upper, swap(lower)).astype(BF)
        pack[2 * pair + 1, rows:, :] = jnp.where(low_part, swap(upper), lower).astype(BF)
    exchange = spread("tm", tm, pack, held, send_h, recv_h, own_h)
    hot, slots = slots_of(routes_ref[...], dp)
    count = dp * CAP_PAD
    spots = lax.broadcasted_iota(jnp.int32, (count, rows), 0).astype(F32)
    placing[...] = ((slots[0] == spots) | (slots[1] == spots)).astype(F32).astype(BF)
    numbers[...] = jnp.zeros_like(numbers)
    for k in range(TOPK):
        hots[k] = hot[k]
        numbers[k : k + 1, :] = slots[k]
    for copy in exchange:
        copy.wait()
    gather.event(1)

    scale = scale_ref[me] * 1.4426950408889634
    ends = []
    for r in range(RECS - 1):
        ends.append(lengths_ref[0, r] + (ends[-1] if ends else 0))
    lane = lax.broadcasted_iota(jnp.int32, (rows, 128), 1)
    minus = lane == HEAD_DIM + RECS

    def unpack(block, carry):
        base = pl.multiple_of(block * rows, 32)
        tile = held[block, :rows, :].astype(F32)
        spot = base + lax.broadcasted_iota(jnp.int32, (rows, 128), 0)
        mark = sum((spot >= end).astype(jnp.int32) for end in ends)
        hit = lane == HEAD_DIM + mark
        apart = jnp.where(hit | (lane > HEAD_DIM + RECS), 0.0, -128.0)
        qs[pl.ds(base, rows), :] = jnp.where(low, tile, jnp.where(minus, -1.0, apart)).astype(BF)
        ks[pl.ds(base, rows), :] = jnp.where(
            low, swap(tile), jnp.where(minus | hit, 1.0, 0.0)
        ).astype(BF)
        values = held[block, rows:, :].astype(F32)
        vs[pl.ds(base, part), :] = jnp.where(low_part, values, 1.0).astype(BF)
        vs[pl.ds(base + part, part), :] = jnp.where(low_part, swap(values), 1.0).astype(BF)
        return carry

    lax.fori_loop(0, tm, unpack, 0)
    outs[:EDGE, :] = jnp.zeros((EDGE, 128), BF)
    outs[EDGE + frames :, :] = jnp.zeros((EDGE, 128), BF)

    def deal(block):
        base = pl.multiple_of(block * rows, 32)
        upper = outs[pl.ds(base, half), :].astype(F32)
        lower = outs[pl.ds(base + half, half), :].astype(F32)
        return jnp.where(low_half, upper, swap(lower)).astype(BF)

    def back(distance):
        peer = lax.rem(me + distance, tm)
        return pltpu.make_async_remote_copy(
            src_ref=att.at[peer],
            dst_ref=heads.at[me],
            send_sem=send_a.at[distance - 1],
            recv_sem=recv_a.at[distance - 1],
            device_id={"tm": peer},
            device_id_type=MESH,
        )

    def attend(step, carry):
        base = pl.multiple_of(lax.rem(me + 1 + step, tm) * rows, 32)
        scores = dot(qs[pl.ds(base, rows), :], ks[...], ((1,), (1,)))
        total = dot(jnp.exp2(scores * scale).astype(BF), vs[...])
        outs[pl.ds(EDGE + base, rows), :] = (total / swap(total)).astype(BF)

        @pl.when(step >= 2)
        def _():
            peer = lax.rem(me + step, tm)
            att[peer] = deal(peer)
            back(step).start()

        return carry

    lax.fori_loop(0, tm, attend, 0)
    att[lax.rem(me + 1, tm)] = deal(lax.rem(me + 1, tm))
    back(1).start()
    heads[me] = deal(me)
    place = me * rows - EDGE + lax.broadcasted_iota(jnp.int32, (wide, 128), 0)
    mark = sum((place >= end).astype(jnp.int32) for end in ends)
    label[...] = jnp.where(place < 0, -1, jnp.where(place >= frames, RECS, mark))
    for distance in range(1, tm):
        back(distance).wait()
    gather.event(2)
    for load in later:
        load.wait()

    for top in range(2):
        tiles = []
        for pair in range(HEADS // 2):
            a = heads[2 * pair].astype(F32)
            b = heads[2 * pair + 1].astype(F32)
            if top == 0:
                tiles.append(jnp.where(low_half, a, swap(b)).astype(BF))
            else:
                tiles.append(jnp.where(low_half, swap(a), b).astype(BF))
        first = dot(jnp.concatenate(tiles, axis=1), proj_ref[...])
        first_s[pl.ds(top * half, half), :] = first
        unit = norm_rows(first).astype(BF).astype(F32)
        for column in range(D // 128):
            normed[column, pl.ds(top * half, half), :] = unit[:, column * 128 : column * 128 + 128]

    strip = 256
    group = 32

    def conv_rows(step, carry):
        base = pl.multiple_of(step * group, group)
        own = label[pl.ds(base + EDGE, group), :]
        for column in range(D // strip):
            total = [jnp.zeros((group, 128), F32)] * (strip // 128)
            for tap in range(KERNEL):
                shift = tap + EDGE - HALF
                same = label[pl.ds(base + shift, group), :] == own
                for n in range(strip // 128):
                    lanes = slice(column * strip + 128 * n, column * strip + 128 * n + 128)
                    value = normed[column * (strip // 128) + n, pl.ds(base + shift, group), :]
                    total[n] = total[n] + jnp.where(same, value * taps_ref[tap : tap + 1, lanes], 0.0)
            for n in range(strip // 128):
                lanes = slice(column * strip + 128 * n, column * strip + 128 * n + 128)
                second[pl.ds(base, group), lanes] = first_s[
                    pl.ds(base + EDGE, group), lanes
                ] + total[n] / (1.0 + jnp.exp(-total[n]))

        @pl.when(step == 5)
        def _():
            gather.event(3)

        return carry

    lax.fori_loop(0, rows // group, conv_rows, 0)

    mixed = norm_rows(second[...]).astype(BF)
    powers = jnp.exp(dot(router_ref[...], mixed, ((1,), (1,))))
    chosen = [jnp.sum(hots[k] * powers, axis=0, keepdims=True) for k in range(TOPK)]
    whole = chosen[0] + chosen[1]
    for k in range(TOPK):
        numbers[TOPK + k : TOPK + k + 1, :] = chosen[k] / whole
    for expert in range(dp):
        cut = placing[expert * CAP_PAD : (expert + 1) * CAP_PAD, :]
        outgoing[expert] = dot(cut, mixed).astype(BF)
    dispatch = spread("dp", dp, outgoing, arrived, send_b, recv_b, own_b)
    gather.event(4)
    columns = jnp.transpose(numbers[...])
    spots = lax.broadcasted_iota(jnp.int32, (rows, count), 1).astype(F32)
    for k in range(TOPK):
        picking[k] = (columns[:, k : k + 1] == spots).astype(F32).astype(BF)
    gates = [columns[:, TOPK + k : TOPK + k + 1] for k in range(TOPK)]
    for copy in dispatch:
        copy.wait()

    units = w_in.shape[0] * w_in.shape[1]
    chunk = w_in.shape[1]
    for shift in (0, 1, -1, 2, -2, 3, -3, 4):
        if shift == 4:
            gather.event(5)
        pair = [gather.at(gather.own, shift), gather.at(gather.other, shift)]
        weights = jnp.concatenate([w_in[one] for one in pair], axis=0)
        value = dot(arrived[...].reshape(count, D), weights, ((1,), (1,)))
        value = (value / (1.0 + jnp.exp(-value))).astype(BF)
        for n, one in enumerate(pair):
            lanes = pl.ds(pl.multiple_of(one * chunk, chunk), chunk)
            hidden[:, lanes] = value[:, n * chunk : (n + 1) * chunk]
    gather.event(6)
    piece = 512
    team = 4
    results = []
    for turn in range(dp // team):
        base = lax.rem(me_dp // team + 1 + turn, dp // team) * team
        start = pl.multiple_of(base * CAP_PAD, team * CAP_PAD)
        for column in range(D // piece):
            cut = slice(column * piece, (column + 1) * piece)
            weights = w_out[:, :, cut].reshape(units, piece)
            value = dot(hidden[pl.ds(start, team * CAP_PAD), :], weights).astype(BF)
            produced[pl.ds(base, team), :, cut] = value.reshape(team, CAP_PAD, piece)
        for n in range(team):
            if turn == dp // team - 1 and n == 0:
                continue
            peer = base + lax.rem(lax.rem(me_dp, team) + n, team)
            distance = lax.rem(peer - me_dp + dp, dp)
            copy = pltpu.make_async_remote_copy(
                src_ref=produced.at[peer],
                dst_ref=returned.at[me_dp],
                send_sem=send_c.at[distance - 1],
                recv_sem=recv_c.at[distance - 1],
                device_id={"dp": peer},
                device_id_type=MESH,
            )
            copy.start()
            results.append(copy)
    returned[me_dp] = produced[me_dp]
    gather.finish()
    for copy in results:
        copy.wait()
    for column in range(D // piece):
        cut = slice(column * piece, (column + 1) * piece)
        value = returned[:, :, cut].reshape(count, piece)
        mixture = gates[0] * dot(picking[0], value) + gates[1] * dot(picking[1], value)
        out_ref[:, cut] = (second[:, cut] + 0.5 * mixture).astype(BF)


def sems(count):
    return [pltpu.SemaphoreType.DMA((count,))] * 2


def body(
    query_rows,
    key_rows,
    value_rows,
    head_scale,
    out_proj,
    conv_taps,
    router,
    expert_in,
    expert_out,
    lengths,
    routes,
):
    rows = query_rows.shape[1]
    tm = lax.axis_size("tm")
    dp = lax.axis_size("dp")
    frames = rows * tm
    wide = rows + 2 * EDGE
    stacked = rows + rows // 2
    chunk = expert_in.shape[1]
    bf = lambda *shape: pltpu.VMEM(shape, BF)
    out = pl.pallas_call(
        functools.partial(block_kernel, tm, dp),
        out_shape=jax.ShapeDtypeStruct((rows, D), BF),
        in_specs=[smem_spec()] * 2 + [vmem_spec()] * 3 + [any_spec()] * 2 + [vmem_spec()] * 2 + [any_spec()] * 2,
        out_specs=vmem_spec(),
        scratch_shapes=[
            bf(tm, stacked, 128),
            bf(tm, stacked, 128),
            bf(frames, 128),
            bf(frames, 128),
            bf(frames, 128),
            bf(frames + 2 * EDGE, 128),
            bf(tm, wide // 2, 128),
            bf(tm, wide // 2, 128),
            pltpu.VMEM((wide, D), F32),
            pltpu.VMEM((D // 128, wide, 128), F32),
            pltpu.VMEM((wide, 128), jnp.int32),
            pltpu.VMEM((rows, D), F32),
            bf(dp, CAP_PAD, D),
            bf(dp, CAP_PAD, D),
            bf(tm, chunk, D),
            bf(tm, chunk, D),
            bf(dp * CAP_PAD, tm * chunk),
            bf(dp, CAP_PAD, D),
            bf(dp, CAP_PAD, D),
            bf(dp * CAP_PAD, rows),
            bf(TOPK, rows, dp * CAP_PAD),
            pltpu.VMEM((TOPK, dp, rows), F32),
            pltpu.VMEM((8, rows), F32),
            bf(*out_proj.shape),
            pltpu.VMEM(conv_taps.shape, F32),
        ]
        + sems(GATHER_IDS)
        + [pltpu.SemaphoreType.DMA((4,))]
        + sems(tm - 1)
        + [pltpu.SemaphoreType.DMA]
        + sems(tm - 1)
        + sems(dp - 1)
        + [pltpu.SemaphoreType.DMA]
        + sems(dp - 1),
        compiler_params=pltpu.CompilerParams(
            vmem_limit_bytes=VMEM_LIMIT, collective_id=0, has_side_effects=True
        ),
        name="block",
    )(
        head_scale,
        lengths,
        query_rows[0],
        key_rows[0],
        value_rows[0],
        out_proj,
        conv_taps,
        router.T,
        routes[0].T,
        expert_in,
        expert_out,
    )
    return out[None]


def solution(mesh):
    return jax.shard_map(
        body,
        mesh=mesh,
        in_specs=(
            P("dp", "tm", None),
            P("dp", "tm", None),
            P("dp", "tm", None),
            P(),
            P(),
            P(),
            P(),
            P("dp", "tm", None),
            P("dp", "tm", None),
            P("dp", None),
            P("dp", "tm", None),
        ),
        out_specs=P("dp", "tm", None),
        check_vma=False,
    )
```

```python
import functools

import jax
import jax.numpy as jnp
from jax import lax
from jax.experimental import pallas as pl
from jax.experimental.pallas import tpu as pltpu
from jax.sharding import PartitionSpec as P

D = 1536
HEADS = 16
HEAD_DIM = 64
KERNEL = 31
HALF = 15
TOPK = 2
RECS = 4
EDGE = 16
CAP_PAD = 48
MESH = pl.DeviceIdType.MESH
BF = jnp.bfloat16
F32 = jnp.float32
VMEM_LIMIT = 60 * 1024 * 1024


def any_spec():
    return pl.BlockSpec(memory_space=pl.ANY)


def vmem_spec():
    return pl.BlockSpec(memory_space=pltpu.VMEM)


def smem_spec():
    return pl.BlockSpec(memory_space=pltpu.SMEM)


def dot(a, b, dims=((1,), (0,))):
    return lax.dot_general(a, b, (dims, ((), ())), preferred_element_type=F32)


def greet(axis, count):
    barrier = pltpu.get_barrier_semaphore()
    me = lax.axis_index(axis)
    for step in range(1, count):
        pl.semaphore_signal(
            barrier, inc=1, device_id={axis: lax.rem(me + step, count)}, device_id_type=MESH
        )


def greeted(total):
    pl.semaphore_wait(pltpu.get_barrier_semaphore(), total)


def spread(axis, count, source, target, send_sem, recv_sem, own_sem):
    me = lax.axis_index(axis)
    copies = []
    for step in range(1, count):
        peer = lax.rem(me + step, count)
        copy = pltpu.make_async_remote_copy(
            src_ref=source.at[peer],
            dst_ref=target.at[me],
            send_sem=send_sem.at[step - 1],
            recv_sem=recv_sem.at[step - 1],
            device_id={axis: peer},
            device_id_type=MESH,
        )
        copy.start()
        copies.append(copy)
    own = pltpu.make_async_copy(source.at[me], target.at[me], own_sem)
    own.start()
    copies.append(own)
    return copies


def low_lanes(shape):
    return lax.broadcasted_iota(jnp.int32, shape, 1) < HEAD_DIM


def pair_ones():
    row = lax.broadcasted_iota(jnp.int32, (128, 128), 0) // HEAD_DIM
    col = lax.broadcasted_iota(jnp.int32, (128, 128), 1) // HEAD_DIM
    return (row == col).astype(F32).astype(BF)


def unit_pair(tile, ones):
    square = tile * tile
    high = square.astype(BF)
    rest = (square - high.astype(F32)).astype(BF)
    total = dot(high, ones) + dot(rest, ones)
    return tile * lax.rsqrt(total + 1e-06)


def swap(tile):
    return pltpu.roll(tile, HEAD_DIM, 1)


def norm_rows(values):
    centered = values - jnp.mean(values, axis=-1, keepdims=True)
    spread_of = jnp.mean(centered * centered, axis=-1, keepdims=True)
    return centered * lax.rsqrt(spread_of + 1e-05)


def slots_of(routes, experts):
    rows = routes.shape[1]
    expert = lax.broadcasted_iota(jnp.int32, (experts, rows), 0)
    hot = [(routes[k : k + 1, :] == expert).astype(F32) for k in range(TOPK)]
    picks = (hot[0] + hot[1]).astype(BF)
    earlier = lax.broadcasted_iota(jnp.int32, (rows, rows), 0) < lax.broadcasted_iota(
        jnp.int32, (rows, rows), 1
    )
    ranks = dot(picks, earlier.astype(F32).astype(BF))
    slots = [
        routes[k : k + 1, :].astype(F32) * CAP_PAD + jnp.sum(hot[k] * ranks, axis=0, keepdims=True)
        for k in range(TOPK)
    ]
    return hot, slots


GATHER_IDS = 30
HOPS = 4


class Gather:
    def __init__(self, w_in, w_out, send_sem, recv_sem):
        self.w_in, self.w_out = w_in, w_out
        self.send_sem, self.recv_sem = send_sem, recv_sem
        self.me = lax.axis_index("tm")
        self.own = self.me // 8 * 8
        self.other = 8 - self.own
        self.z = self.me - self.own

    def at(self, base, shift):
        return base + lax.rem(self.z + shift + 8, 8)

    def table(self):
        w_in, w_out, own, other, at = self.w_in, self.w_out, self.own, self.other, self.at
        up, down, across = at(own, 1), at(own, -1), at(other, 0)
        table = {0: (w_in, self.me, across, across), 1: (w_out, self.me, across, across)}
        for h in range(1, HOPS + 1):
            table[1 + h] = (w_out, at(own, -h), across, at(other, -h))
            table[8 + h] = (w_out, at(own, 1 - h), up, at(own, -h))
            table[15 + h] = (w_in, at(own, 1 - h), up, at(own, -h))
            table[25 + h] = (w_in, at(other, h - 1), down, at(other, h))
        for h in range(1, HOPS):
            table[5 + h] = (w_out, at(own, h), across, at(other, h))
            table[12 + h] = (w_out, at(own, h - 1), down, at(own, h))
            table[19 + h] = (w_in, at(other, 1 - h), up, at(other, -h))
            table[22 + h] = (w_in, at(own, h - 1), down, at(own, h))
        return table

    def copy(self, n, chunk):
        buffer, _, peer, _ = self.table()[n]
        return pltpu.make_async_remote_copy(
            src_ref=buffer.at[chunk],
            dst_ref=buffer.at[chunk],
            send_sem=self.send_sem.at[n],
            recv_sem=self.recv_sem.at[n],
            device_id={"tm": peer},
            device_id_type=MESH,
        )

    def start(self, *ids):
        for n in ids:
            self.copy(n, self.table()[n][1]).start()

    def receive(self, *ids):
        for n in ids:
            self.copy(n, self.table()[n][3]).wait_recv()

    def finish(self):
        for n in range(GATHER_IDS):
            self.copy(n, self.table()[n][1]).wait_send()

    def event(self, n):
        if n == 0:
            self.start(1, 0, 9, 13)
        elif n == 1:
            self.receive(9, 13)
            self.start(10, 14, 2, 6)
        elif n == 2:
            self.receive(10, 14)
            self.start(11, 15, 3, 7, 16, 23)
        elif n == 3:
            self.receive(11, 15)
            self.start(12)
            self.receive(0)
            self.start(20, 26)
        elif n == 4:
            self.start(4, 8)
            self.receive(16, 23)
            self.start(17, 24)
        elif n == 5:
            self.receive(12)
            self.start(5)
            self.receive(20, 26)
            self.start(21, 27)
        elif n == 6:
            self.receive(17, 24)
            self.start(18, 25)
            self.receive(21, 27)
            self.start(22, 28)
            self.receive(18, 25)
            self.start(19)
            self.receive(22, 28)
            self.start(29)
        elif n == 7:
            self.receive(19, 29)
        else:
            self.receive(1, 2, 3, 4, 5, 6, 7, 8)


def block_kernel(
    tm,
    dp,
    scale_ref,
    lengths_ref,
    q_ref,
    k_ref,
    v_ref,
    proj_hbm,
    taps_hbm,
    router_ref,
    routes_ref,
    in_ref,
    out_w_ref,
    out_ref,
    pack,
    held,
    qs,
    ks,
    vs,
    outs,
    att,
    heads,
    first_s,
    normed,
    label,
    second,
    outgoing,
    arrived,
    w_in,
    w_out,
    hidden,
    produced,
    returned,
    placing,
    picking,
    hots,
    numbers,
    proj_ref,
    taps_ref,
    gather_send,
    gather_recv,
    load_sem,
    send_h,
    recv_h,
    own_h,
    send_a,
    recv_a,
    send_b,
    recv_b,
    own_b,
    send_c,
    recv_c,
):
    greet("tm", tm)
    greet("dp", dp)
    me = lax.axis_index("tm")
    me_dp = lax.axis_index("dp")
    rows = q_ref.shape[0]
    frames = rows * tm
    part = rows // 2
    wide = rows + 2 * EDGE
    half = wide // 2
    gather = Gather(w_in, w_out, gather_send, gather_recv)
    loads = [
        pltpu.make_async_copy(in_ref.at[0], w_in.at[me], load_sem.at[0]),
        pltpu.make_async_copy(out_w_ref.at[0], w_out.at[me], load_sem.at[1]),
    ]
    later = [
        pltpu.make_async_copy(proj_hbm, proj_ref, load_sem.at[2]),
        pltpu.make_async_copy(taps_hbm, taps_ref, load_sem.at[3]),
    ]
    for load in loads + later:
        load.start()
    for load in loads:
        load.wait()
    greeted(tm + dp - 2)
    gather.event(0)

    ones = pair_ones()
    low = low_lanes((rows, 128))
    low_part = low_lanes((part, 128))
    low_half = low_lanes((half, 128))
    for pair in range(HEADS // 2):
        lanes = slice(128 * pair, 128 * pair + 128)
        q = unit_pair(q_ref[:, lanes].astype(F32), ones)
        k = unit_pair(k_ref[:, lanes].astype(F32), ones)
        pack[2 * pair, :rows, :] = jnp.where(low, q, swap(k)).astype(BF)
        pack[2 * pair + 1, :rows, :] = jnp.where(low, swap(q), k).astype(BF)
        upper = v_ref[:part, lanes].astype(F32)
        lower = v_ref[part:, lanes].astype(F32)
        pack[2 * pair, rows:, :] = jnp.where(low_part, upper, swap(lower)).astype(BF)
        pack[2 * pair + 1, rows:, :] = jnp.where(low_part, swap(upper), lower).astype(BF)
    exchange = spread("tm", tm, pack, held, send_h, recv_h, own_h)
    hot, slots = slots_of(routes_ref[...], dp)
    count = dp * CAP_PAD
    spots = lax.broadcasted_iota(jnp.int32, (count, rows), 0).astype(F32)
    placing[...] = ((slots[0] == spots) | (slots[1] == spots)).astype(F32).astype(BF)
    numbers[...] = jnp.zeros_like(numbers)
    for k in range(TOPK):
        hots[k] = hot[k]
        numbers[k : k + 1, :] = slots[k]
    for copy in exchange:
        copy.wait()
    gather.event(1)

    scale = scale_ref[me] * 1.4426950408889634
    ends = []
    for r in range(RECS - 1):
        ends.append(lengths_ref[0, r] + (ends[-1] if ends else 0))
    lane = lax.broadcasted_iota(jnp.int32, (rows, 128), 1)
    minus = lane == HEAD_DIM + RECS

    def unpack(block, carry):
        base = pl.multiple_of(block * rows, 32)
        tile = held[block, :rows, :].astype(F32)
        spot = base + lax.broadcasted_iota(jnp.int32, (rows, 128), 0)
        mark = sum((spot >= end).astype(jnp.int32) for end in ends)
        hit = lane == HEAD_DIM + mark
        apart = jnp.where(hit | (lane > HEAD_DIM + RECS), 0.0, -128.0)
        qs[pl.ds(base, rows), :] = jnp.where(low, tile, jnp.where(minus, -1.0, apart)).astype(BF)
        ks[pl.ds(base, rows), :] = jnp.where(
            low, swap(tile), jnp.where(minus | hit, 1.0, 0.0)
        ).astype(BF)
        values = held[block, rows:, :].astype(F32)
        vs[pl.ds(base, part), :] = jnp.where(low_part, values, 1.0).astype(BF)
        vs[pl.ds(base + part, part), :] = jnp.where(low_part, swap(values), 1.0).astype(BF)
        return carry

    lax.fori_loop(0, tm, unpack, 0)
    outs[:EDGE, :] = jnp.zeros((EDGE, 128), BF)
    outs[EDGE + frames :, :] = jnp.zeros((EDGE, 128), BF)

    def deal(block):
        base = pl.multiple_of(block * rows, 32)
        upper = outs[pl.ds(base, half), :].astype(F32)
        lower = outs[pl.ds(base + half, half), :].astype(F32)
        return jnp.where(low_half, upper, swap(lower)).astype(BF)

    def back(distance):
        peer = lax.rem(me + distance, tm)
        return pltpu.make_async_remote_copy(
            src_ref=att.at[peer],
            dst_ref=heads.at[me],
            send_sem=send_a.at[distance - 1],
            recv_sem=recv_a.at[distance - 1],
            device_id={"tm": peer},
            device_id_type=MESH,
        )

    def attend(step, carry):
        base = pl.multiple_of(lax.rem(me + 1 + step, tm) * rows, 32)
        scores = dot(qs[pl.ds(base, rows), :], ks[...], ((1,), (1,)))
        total = dot(jnp.exp2(scores * scale).astype(BF), vs[...])
        outs[pl.ds(EDGE + base, rows), :] = (total / swap(total)).astype(BF)

        @pl.when(step >= 2)
        def _():
            peer = lax.rem(me + step, tm)
            att[peer] = deal(peer)
            back(step).start()

        @pl.when(step == 5)
        def _():
            gather.event(2)

        @pl.when(step == 12)
        def _():
            gather.event(3)

        return carry

    lax.fori_loop(0, tm, attend, 0)
    att[lax.rem(me + 1, tm)] = deal(lax.rem(me + 1, tm))
    back(1).start()
    heads[me] = deal(me)
    gather.event(4)
    place = me * rows - EDGE + lax.broadcasted_iota(jnp.int32, (wide, 128), 0)
    mark = sum((place >= end).astype(jnp.int32) for end in ends)
    label[...] = jnp.where(place < 0, -1, jnp.where(place >= frames, RECS, mark))
    for distance in range(1, tm):
        back(distance).wait()
    gather.event(5)
    for load in later:
        load.wait()

    for top in range(2):
        tiles = []
        for pair in range(HEADS // 2):
            a = heads[2 * pair].astype(F32)
            b = heads[2 * pair + 1].astype(F32)
            if top == 0:
                tiles.append(jnp.where(low_half, a, swap(b)).astype(BF))
            else:
                tiles.append(jnp.where(low_half, swap(a), b).astype(BF))
        first = dot(jnp.concatenate(tiles, axis=1), proj_ref[...])
        first_s[pl.ds(top * half, half), :] = first
        unit = norm_rows(first).astype(BF).astype(F32)
        for column in range(D // 128):
            normed[column, pl.ds(top * half, half), :] = unit[:, column * 128 : column * 128 + 128]

    strip = 256
    group = 32

    def conv_rows(step, carry):
        base = pl.multiple_of(step * group, group)
        own = label[pl.ds(base + EDGE, group), :]
        for column in range(D // strip):
            total = [jnp.zeros((group, 128), F32)] * (strip // 128)
            for tap in range(KERNEL):
                shift = tap + EDGE - HALF
                same = label[pl.ds(base + shift, group), :] == own
                for n in range(strip // 128):
                    lanes = slice(column * strip + 128 * n, column * strip + 128 * n + 128)
                    value = normed[column * (strip // 128) + n, pl.ds(base + shift, group), :]
                    total[n] = total[n] + jnp.where(same, value * taps_ref[tap : tap + 1, lanes], 0.0)
            for n in range(strip // 128):
                lanes = slice(column * strip + 128 * n, column * strip + 128 * n + 128)
                second[pl.ds(base, group), lanes] = first_s[
                    pl.ds(base + EDGE, group), lanes
                ] + total[n] / (1.0 + jnp.exp(-total[n]))

        return carry

    lax.fori_loop(0, rows // group, conv_rows, 0)

    mixed = norm_rows(second[...]).astype(BF)
    powers = jnp.exp(dot(router_ref[...], mixed, ((1,), (1,))))
    chosen = [jnp.sum(hots[k] * powers, axis=0, keepdims=True) for k in range(TOPK)]
    whole = chosen[0] + chosen[1]
    for k in range(TOPK):
        numbers[TOPK + k : TOPK + k + 1, :] = chosen[k] / whole
    for expert in range(dp):
        cut = placing[expert * CAP_PAD : (expert + 1) * CAP_PAD, :]
        outgoing[expert] = dot(cut, mixed).astype(BF)
    dispatch = spread("dp", dp, outgoing, arrived, send_b, recv_b, own_b)
    gather.event(6)
    columns = jnp.transpose(numbers[...])
    spots = lax.broadcasted_iota(jnp.int32, (rows, count), 1).astype(F32)
    for k in range(TOPK):
        picking[k] = (columns[:, k : k + 1] == spots).astype(F32).astype(BF)
    gates = [columns[:, TOPK + k : TOPK + k + 1] for k in range(TOPK)]
    for copy in dispatch:
        copy.wait()

    units = w_in.shape[0] * w_in.shape[1]
    chunk = w_in.shape[1]
    for shift in (0, 1, -1, 2, -2, 3, -3, 4):
        if shift == 4:
            gather.event(7)
        pair = [gather.at(gather.own, shift), gather.at(gather.other, shift)]
        weights = jnp.concatenate([w_in[one] for one in pair], axis=0)
        value = dot(arrived[...].reshape(count, D), weights, ((1,), (1,)))
        value = (value / (1.0 + jnp.exp(-value))).astype(BF)
        for n, one in enumerate(pair):
            lanes = pl.ds(pl.multiple_of(one * chunk, chunk), chunk)
            hidden[:, lanes] = value[:, n * chunk : (n + 1) * chunk]
    gather.event(8)
    piece = 512
    team = 4
    results = []
    for turn in range(dp // team):
        base = lax.rem(me_dp // team + 1 + turn, dp // team) * team
        start = pl.multiple_of(base * CAP_PAD, team * CAP_PAD)
        for column in range(D // piece):
            cut = slice(column * piece, (column + 1) * piece)
            weights = w_out[:, :, cut].reshape(units, piece)
            value = dot(hidden[pl.ds(start, team * CAP_PAD), :], weights).astype(BF)
            produced[pl.ds(base, team), :, cut] = value.reshape(team, CAP_PAD, piece)
        for n in range(team):
            if turn == dp // team - 1 and n == 0:
                continue
            peer = base + lax.rem(lax.rem(me_dp, team) + n, team)
            distance = lax.rem(peer - me_dp + dp, dp)
            copy = pltpu.make_async_remote_copy(
                src_ref=produced.at[peer],
                dst_ref=returned.at[me_dp],
                send_sem=send_c.at[distance - 1],
                recv_sem=recv_c.at[distance - 1],
                device_id={"dp": peer},
                device_id_type=MESH,
            )
            copy.start()
            results.append(copy)
    returned[me_dp] = produced[me_dp]
    gather.finish()
    for copy in results:
        copy.wait()
    for column in range(D // piece):
        cut = slice(column * piece, (column + 1) * piece)
        value = returned[:, :, cut].reshape(count, piece)
        mixture = gates[0] * dot(picking[0], value) + gates[1] * dot(picking[1], value)
        out_ref[:, cut] = (second[:, cut] + 0.5 * mixture).astype(BF)


def sems(count):
    return [pltpu.SemaphoreType.DMA((count,))] * 2


def body(
    query_rows,
    key_rows,
    value_rows,
    head_scale,
    out_proj,
    conv_taps,
    router,
    expert_in,
    expert_out,
    lengths,
    routes,
):
    rows = query_rows.shape[1]
    tm = lax.axis_size("tm")
    dp = lax.axis_size("dp")
    frames = rows * tm
    wide = rows + 2 * EDGE
    stacked = rows + rows // 2
    chunk = expert_in.shape[1]
    bf = lambda *shape: pltpu.VMEM(shape, BF)
    out = pl.pallas_call(
        functools.partial(block_kernel, tm, dp),
        out_shape=jax.ShapeDtypeStruct((rows, D), BF),
        in_specs=[smem_spec()] * 2 + [vmem_spec()] * 3 + [any_spec()] * 2 + [vmem_spec()] * 2 + [any_spec()] * 2,
        out_specs=vmem_spec(),
        scratch_shapes=[
            bf(tm, stacked, 128),
            bf(tm, stacked, 128),
            bf(frames, 128),
            bf(frames, 128),
            bf(frames, 128),
            bf(frames + 2 * EDGE, 128),
            bf(tm, wide // 2, 128),
            bf(tm, wide // 2, 128),
            pltpu.VMEM((wide, D), F32),
            pltpu.VMEM((D // 128, wide, 128), F32),
            pltpu.VMEM((wide, 128), jnp.int32),
            pltpu.VMEM((rows, D), F32),
            bf(dp, CAP_PAD, D),
            bf(dp, CAP_PAD, D),
            bf(tm, chunk, D),
            bf(tm, chunk, D),
            bf(dp * CAP_PAD, tm * chunk),
            bf(dp, CAP_PAD, D),
            bf(dp, CAP_PAD, D),
            bf(dp * CAP_PAD, rows),
            bf(TOPK, rows, dp * CAP_PAD),
            pltpu.VMEM((TOPK, dp, rows), F32),
            pltpu.VMEM((8, rows), F32),
            bf(*out_proj.shape),
            pltpu.VMEM(conv_taps.shape, F32),
        ]
        + sems(GATHER_IDS)
        + [pltpu.SemaphoreType.DMA((4,))]
        + sems(tm - 1)
        + [pltpu.SemaphoreType.DMA]
        + sems(tm - 1)
        + sems(dp - 1)
        + [pltpu.SemaphoreType.DMA]
        + sems(dp - 1),
        compiler_params=pltpu.CompilerParams(
            vmem_limit_bytes=VMEM_LIMIT, collective_id=0, has_side_effects=True
        ),
        name="block",
    )(
        head_scale,
        lengths,
        query_rows[0],
        key_rows[0],
        value_rows[0],
        out_proj,
        conv_taps,
        router.T,
        routes[0].T,
        expert_in,
        expert_out,
    )
    return out[None]


def solution(mesh):
    return jax.shard_map(
        body,
        mesh=mesh,
        in_specs=(
            P("dp", "tm", None),
            P("dp", "tm", None),
            P("dp", "tm", None),
            P(),
            P(),
            P(),
            P(),
            P("dp", "tm", None),
            P("dp", "tm", None),
            P("dp", None),
            P("dp", "tm", None),
        ),
        out_specs=P("dp", "tm", None),
        check_vma=False,
    )
```

```python
import functools

import jax
import jax.numpy as jnp
from jax import lax
from jax.experimental import pallas as pl
from jax.experimental.pallas import tpu as pltpu
from jax.sharding import PartitionSpec as P

D = 1536
HEADS = 16
HEAD_DIM = 64
KERNEL = 31
HALF = 15
TOPK = 2
RECS = 4
EDGE = 16
CAP_PAD = 48
MESH = pl.DeviceIdType.MESH
BF = jnp.bfloat16
F32 = jnp.float32
VMEM_LIMIT = 60 * 1024 * 1024


def any_spec():
    return pl.BlockSpec(memory_space=pl.ANY)


def vmem_spec():
    return pl.BlockSpec(memory_space=pltpu.VMEM)


def smem_spec():
    return pl.BlockSpec(memory_space=pltpu.SMEM)


def dot(a, b, dims=((1,), (0,))):
    return lax.dot_general(a, b, (dims, ((), ())), preferred_element_type=F32)


def greet(axis, count):
    barrier = pltpu.get_barrier_semaphore()
    me = lax.axis_index(axis)
    for step in range(1, count):
        pl.semaphore_signal(
            barrier, inc=1, device_id={axis: lax.rem(me + step, count)}, device_id_type=MESH
        )


def greeted(total):
    pl.semaphore_wait(pltpu.get_barrier_semaphore(), total)


def spread(axis, count, source, target, send_sem, recv_sem, own_sem):
    me = lax.axis_index(axis)
    copies = []
    for step in range(1, count):
        peer = lax.rem(me + step, count)
        copy = pltpu.make_async_remote_copy(
            src_ref=source.at[peer],
            dst_ref=target.at[me],
            send_sem=send_sem.at[step - 1],
            recv_sem=recv_sem.at[step - 1],
            device_id={axis: peer},
            device_id_type=MESH,
        )
        copy.start()
        copies.append(copy)
    own = pltpu.make_async_copy(source.at[me], target.at[me], own_sem)
    own.start()
    copies.append(own)
    return copies


def low_lanes(shape):
    return lax.broadcasted_iota(jnp.int32, shape, 1) < HEAD_DIM


def pair_ones():
    row = lax.broadcasted_iota(jnp.int32, (128, 128), 0) // HEAD_DIM
    col = lax.broadcasted_iota(jnp.int32, (128, 128), 1) // HEAD_DIM
    return (row == col).astype(F32).astype(BF)


def unit_pair(tile, ones):
    square = tile * tile
    high = square.astype(BF)
    rest = (square - high.astype(F32)).astype(BF)
    total = dot(high, ones) + dot(rest, ones)
    return tile * lax.rsqrt(total + 1e-06)


def swap(tile):
    return pltpu.roll(tile, HEAD_DIM, 1)


def norm_rows(values):
    centered = values - jnp.mean(values, axis=-1, keepdims=True)
    spread_of = jnp.mean(centered * centered, axis=-1, keepdims=True)
    return centered * lax.rsqrt(spread_of + 1e-05)


def slots_of(routes, experts):
    rows = routes.shape[1]
    expert = lax.broadcasted_iota(jnp.int32, (experts, rows), 0)
    hot = [(routes[k : k + 1, :] == expert).astype(F32) for k in range(TOPK)]
    picks = (hot[0] + hot[1]).astype(BF)
    earlier = lax.broadcasted_iota(jnp.int32, (rows, rows), 0) < lax.broadcasted_iota(
        jnp.int32, (rows, rows), 1
    )
    ranks = dot(picks, earlier.astype(F32).astype(BF))
    slots = [
        routes[k : k + 1, :].astype(F32) * CAP_PAD + jnp.sum(hot[k] * ranks, axis=0, keepdims=True)
        for k in range(TOPK)
    ]
    return hot, slots


GATHER_IDS = 30
HOPS = 4


class Gather:
    def __init__(self, w_in, w_out, send_sem, recv_sem):
        self.w_in, self.w_out = w_in, w_out
        self.send_sem, self.recv_sem = send_sem, recv_sem
        self.me = lax.axis_index("tm")
        self.own = self.me // 8 * 8
        self.other = 8 - self.own
        self.z = self.me - self.own

    def at(self, base, shift):
        return base + lax.rem(self.z + shift + 8, 8)

    def table(self):
        w_in, w_out, own, other, at = self.w_in, self.w_out, self.own, self.other, self.at
        up, down, across = at(own, 1), at(own, -1), at(other, 0)
        table = {0: (w_in, self.me, across, across), 1: (w_out, self.me, across, across)}
        for h in range(1, HOPS + 1):
            table[1 + h] = (w_out, at(own, -h), across, at(other, -h))
            table[8 + h] = (w_out, at(own, 1 - h), up, at(own, -h))
            table[15 + h] = (w_in, at(own, 1 - h), up, at(own, -h))
            table[25 + h] = (w_in, at(other, h - 1), down, at(other, h))
        for h in range(1, HOPS):
            table[5 + h] = (w_out, at(own, h), across, at(other, h))
            table[12 + h] = (w_out, at(own, h - 1), down, at(own, h))
            table[19 + h] = (w_in, at(other, 1 - h), up, at(other, -h))
            table[22 + h] = (w_in, at(own, h - 1), down, at(own, h))
        return table

    def copy(self, n, chunk):
        buffer, _, peer, _ = self.table()[n]
        return pltpu.make_async_remote_copy(
            src_ref=buffer.at[chunk],
            dst_ref=buffer.at[chunk],
            send_sem=self.send_sem.at[n],
            recv_sem=self.recv_sem.at[n],
            device_id={"tm": peer},
            device_id_type=MESH,
        )

    def start(self, *ids):
        for n in ids:
            self.copy(n, self.table()[n][1]).start()

    def receive(self, *ids):
        for n in ids:
            self.copy(n, self.table()[n][3]).wait_recv()

    def finish(self):
        for n in range(GATHER_IDS):
            self.copy(n, self.table()[n][1]).wait_send()

    def event(self, n):
        if n == 0:
            self.start(1, 0, 9, 13)
        elif n == 1:
            self.receive(9, 13)
            self.start(10, 14, 2, 6)
        elif n == 2:
            self.receive(10, 14)
            self.start(11, 15, 3, 7, 16, 23)
        elif n == 3:
            self.receive(11, 15)
            self.start(12, 4, 8)
            self.receive(0)
            self.start(20, 26)
        elif n == 4:
            self.receive(16, 23)
            self.start(17, 24)
        elif n == 5:
            self.receive(12)
            self.start(5)
            self.receive(20, 26)
            self.start(21, 27)
        elif n == 9:
            self.receive(17, 24)
            self.start(18, 25)
        elif n == 6:
            self.receive(21, 27)
            self.start(22, 28)
            self.receive(18, 25)
            self.start(19)
            self.receive(22, 28)
            self.start(29)
        elif n == 7:
            self.receive(19, 29)
        else:
            self.receive(1, 2, 3, 4, 5, 6, 7, 8)


def block_kernel(
    tm,
    dp,
    scale_ref,
    lengths_ref,
    q_ref,
    k_ref,
    v_ref,
    proj_hbm,
    taps_hbm,
    router_ref,
    routes_ref,
    in_ref,
    out_w_ref,
    out_ref,
    pack,
    held,
    qs,
    ks,
    vs,
    outs,
    att,
    heads,
    first_s,
    normed,
    label,
    second,
    outgoing,
    arrived,
    w_in,
    w_out,
    hidden,
    produced,
    returned,
    placing,
    picking,
    hots,
    numbers,
    proj_ref,
    taps_ref,
    gather_send,
    gather_recv,
    load_sem,
    send_h,
    recv_h,
    own_h,
    send_a,
    recv_a,
    send_b,
    recv_b,
    own_b,
    send_c,
    recv_c,
):
    greet("tm", tm)
    greet("dp", dp)
    me = lax.axis_index("tm")
    me_dp = lax.axis_index("dp")
    rows = q_ref.shape[0]
    frames = rows * tm
    part = rows // 2
    wide = rows + 2 * EDGE
    half = wide // 2
    gather = Gather(w_in, w_out, gather_send, gather_recv)
    loads = [
        pltpu.make_async_copy(in_ref.at[0], w_in.at[me], load_sem.at[0]),
        pltpu.make_async_copy(out_w_ref.at[0], w_out.at[me], load_sem.at[1]),
    ]
    later = [
        pltpu.make_async_copy(proj_hbm, proj_ref, load_sem.at[2]),
        pltpu.make_async_copy(taps_hbm, taps_ref, load_sem.at[3]),
    ]
    for load in loads + later:
        load.start()
    for load in loads:
        load.wait()
    greeted(tm + dp - 2)
    gather.event(0)

    ones = pair_ones()
    low = low_lanes((rows, 128))
    low_part = low_lanes((part, 128))
    low_half = low_lanes((half, 128))
    for pair in range(HEADS // 2):
        lanes = slice(128 * pair, 128 * pair + 128)
        q = unit_pair(q_ref[:, lanes].astype(F32), ones)
        k = unit_pair(k_ref[:, lanes].astype(F32), ones)
        pack[2 * pair, :rows, :] = jnp.where(low, q, swap(k)).astype(BF)
        pack[2 * pair + 1, :rows, :] = jnp.where(low, swap(q), k).astype(BF)
        upper = v_ref[:part, lanes].astype(F32)
        lower = v_ref[part:, lanes].astype(F32)
        pack[2 * pair, rows:, :] = jnp.where(low_part, upper, swap(lower)).astype(BF)
        pack[2 * pair + 1, rows:, :] = jnp.where(low_part, swap(upper), lower).astype(BF)
    exchange = spread("tm", tm, pack, held, send_h, recv_h, own_h)
    hot, slots = slots_of(routes_ref[...], dp)
    count = dp * CAP_PAD
    spots = lax.broadcasted_iota(jnp.int32, (count, rows), 0).astype(F32)
    placing[...] = ((slots[0] == spots) | (slots[1] == spots)).astype(F32).astype(BF)
    numbers[...] = jnp.zeros_like(numbers)
    for k in range(TOPK):
        hots[k] = hot[k]
        numbers[k : k + 1, :] = slots[k]
    for copy in exchange:
        copy.wait()
    gather.event(1)

    scale = scale_ref[me] * 1.4426950408889634
    ends = []
    for r in range(RECS - 1):
        ends.append(lengths_ref[0, r] + (ends[-1] if ends else 0))
    lane = lax.broadcasted_iota(jnp.int32, (rows, 128), 1)
    minus = lane == HEAD_DIM + RECS

    def unpack(block, carry):
        base = pl.multiple_of(block * rows, 32)
        tile = held[block, :rows, :].astype(F32)
        spot = base + lax.broadcasted_iota(jnp.int32, (rows, 128), 0)
        mark = sum((spot >= end).astype(jnp.int32) for end in ends)
        hit = lane == HEAD_DIM + mark
        apart = jnp.where(hit | (lane > HEAD_DIM + RECS), 0.0, -128.0)
        qs[pl.ds(base, rows), :] = jnp.where(low, tile, jnp.where(minus, -1.0, apart)).astype(BF)
        ks[pl.ds(base, rows), :] = jnp.where(
            low, swap(tile), jnp.where(minus | hit, 1.0, 0.0)
        ).astype(BF)
        values = held[block, rows:, :].astype(F32)
        vs[pl.ds(base, part), :] = jnp.where(low_part, values, 1.0).astype(BF)
        vs[pl.ds(base + part, part), :] = jnp.where(low_part, swap(values), 1.0).astype(BF)
        return carry

    lax.fori_loop(0, tm, unpack, 0)
    outs[:EDGE, :] = jnp.zeros((EDGE, 128), BF)
    outs[EDGE + frames :, :] = jnp.zeros((EDGE, 128), BF)

    def deal(block):
        base = pl.multiple_of(block * rows, 32)
        upper = outs[pl.ds(base, half), :].astype(F32)
        lower = outs[pl.ds(base + half, half), :].astype(F32)
        return jnp.where(low_half, upper, swap(lower)).astype(BF)

    def back(distance):
        peer = lax.rem(me + distance, tm)
        return pltpu.make_async_remote_copy(
            src_ref=att.at[peer],
            dst_ref=heads.at[me],
            send_sem=send_a.at[distance - 1],
            recv_sem=recv_a.at[distance - 1],
            device_id={"tm": peer},
            device_id_type=MESH,
        )

    def attend(step, carry):
        base = pl.multiple_of(lax.rem(me + 1 + step, tm) * rows, 32)
        scores = dot(qs[pl.ds(base, rows), :], ks[...], ((1,), (1,)))
        total = dot(jnp.exp2(scores * scale).astype(BF), vs[...])
        outs[pl.ds(EDGE + base, rows), :] = (total / swap(total)).astype(BF)

        @pl.when(step >= 2)
        def _():
            peer = lax.rem(me + step, tm)
            att[peer] = deal(peer)
            back(step).start()

        @pl.when(step == 5)
        def _():
            gather.event(2)

        @pl.when(step == 12)
        def _():
            gather.event(3)

        return carry

    lax.fori_loop(0, tm, attend, 0)
    att[lax.rem(me + 1, tm)] = deal(lax.rem(me + 1, tm))
    back(1).start()
    heads[me] = deal(me)
    gather.event(4)
    place = me * rows - EDGE + lax.broadcasted_iota(jnp.int32, (wide, 128), 0)
    mark = sum((place >= end).astype(jnp.int32) for end in ends)
    label[...] = jnp.where(place < 0, -1, jnp.where(place >= frames, RECS, mark))
    for distance in range(1, tm):
        back(distance).wait()
    gather.event(5)
    for load in later:
        load.wait()

    for top in range(2):
        tiles = []
        for pair in range(HEADS // 2):
            a = heads[2 * pair].astype(F32)
            b = heads[2 * pair + 1].astype(F32)
            if top == 0:
                tiles.append(jnp.where(low_half, a, swap(b)).astype(BF))
            else:
                tiles.append(jnp.where(low_half, swap(a), b).astype(BF))
        first = dot(jnp.concatenate(tiles, axis=1), proj_ref[...])
        first_s[pl.ds(top * half, half), :] = first
        unit = norm_rows(first).astype(BF).astype(F32)
        for column in range(D // 128):
            normed[column, pl.ds(top * half, half), :] = unit[:, column * 128 : column * 128 + 128]

    strip = 256
    group = 32

    def conv_rows(step, carry):
        base = pl.multiple_of(step * group, group)
        own = label[pl.ds(base + EDGE, group), :]
        for column in range(D // strip):
            total = [jnp.zeros((group, 128), F32)] * (strip // 128)
            for tap in range(KERNEL):
                shift = tap + EDGE - HALF
                same = label[pl.ds(base + shift, group), :] == own
                for n in range(strip // 128):
                    lanes = slice(column * strip + 128 * n, column * strip + 128 * n + 128)
                    value = normed[column * (strip // 128) + n, pl.ds(base + shift, group), :]
                    total[n] = total[n] + jnp.where(same, value * taps_ref[tap : tap + 1, lanes], 0.0)
            for n in range(strip // 128):
                lanes = slice(column * strip + 128 * n, column * strip + 128 * n + 128)
                second[pl.ds(base, group), lanes] = first_s[
                    pl.ds(base + EDGE, group), lanes
                ] + total[n] / (1.0 + jnp.exp(-total[n]))

        @pl.when(step == 4)
        def _():
            gather.event(9)

        return carry

    lax.fori_loop(0, rows // group, conv_rows, 0)

    mixed = norm_rows(second[...]).astype(BF)
    powers = jnp.exp(dot(router_ref[...], mixed, ((1,), (1,))))
    chosen = [jnp.sum(hots[k] * powers, axis=0, keepdims=True) for k in range(TOPK)]
    whole = chosen[0] + chosen[1]
    for k in range(TOPK):
        numbers[TOPK + k : TOPK + k + 1, :] = chosen[k] / whole
    for expert in range(dp):
        cut = placing[expert * CAP_PAD : (expert + 1) * CAP_PAD, :]
        outgoing[expert] = dot(cut, mixed).astype(BF)
    dispatch = spread("dp", dp, outgoing, arrived, send_b, recv_b, own_b)
    gather.event(6)
    columns = jnp.transpose(numbers[...])
    spots = lax.broadcasted_iota(jnp.int32, (rows, count), 1).astype(F32)
    for k in range(TOPK):
        picking[k] = (columns[:, k : k + 1] == spots).astype(F32).astype(BF)
    gates = [columns[:, TOPK + k : TOPK + k + 1] for k in range(TOPK)]
    for copy in dispatch:
        copy.wait()

    units = w_in.shape[0] * w_in.shape[1]
    chunk = w_in.shape[1]
    for shift in (0, 1, -1, 2, -2, 3, -3, 4):
        if shift == 4:
            gather.event(7)
        pair = [gather.at(gather.own, shift), gather.at(gather.other, shift)]
        weights = jnp.concatenate([w_in[one] for one in pair], axis=0)
        value = dot(arrived[...].reshape(count, D), weights, ((1,), (1,)))
        value = (value / (1.0 + jnp.exp(-value))).astype(BF)
        for n, one in enumerate(pair):
            lanes = pl.ds(pl.multiple_of(one * chunk, chunk), chunk)
            hidden[:, lanes] = value[:, n * chunk : (n + 1) * chunk]
    gather.event(8)
    piece = 512
    team = 4
    results = []
    for turn in range(dp // team):
        base = lax.rem(me_dp // team + 1 + turn, dp // team) * team
        start = pl.multiple_of(base * CAP_PAD, team * CAP_PAD)
        for column in range(D // piece):
            cut = slice(column * piece, (column + 1) * piece)
            weights = w_out[:, :, cut].reshape(units, piece)
            value = dot(hidden[pl.ds(start, team * CAP_PAD), :], weights).astype(BF)
            produced[pl.ds(base, team), :, cut] = value.reshape(team, CAP_PAD, piece)
        for n in range(team):
            if turn == dp // team - 1 and n == 0:
                continue
            peer = base + lax.rem(lax.rem(me_dp, team) + n, team)
            distance = lax.rem(peer - me_dp + dp, dp)
            copy = pltpu.make_async_remote_copy(
                src_ref=produced.at[peer],
                dst_ref=returned.at[me_dp],
                send_sem=send_c.at[distance - 1],
                recv_sem=recv_c.at[distance - 1],
                device_id={"dp": peer},
                device_id_type=MESH,
            )
            copy.start()
            results.append(copy)
    returned[me_dp] = produced[me_dp]
    gather.finish()
    for copy in results:
        copy.wait()
    for column in range(D // piece):
        cut = slice(column * piece, (column + 1) * piece)
        value = returned[:, :, cut].reshape(count, piece)
        mixture = gates[0] * dot(picking[0], value) + gates[1] * dot(picking[1], value)
        out_ref[:, cut] = (second[:, cut] + 0.5 * mixture).astype(BF)


def sems(count):
    return [pltpu.SemaphoreType.DMA((count,))] * 2


def body(
    query_rows,
    key_rows,
    value_rows,
    head_scale,
    out_proj,
    conv_taps,
    router,
    expert_in,
    expert_out,
    lengths,
    routes,
):
    rows = query_rows.shape[1]
    tm = lax.axis_size("tm")
    dp = lax.axis_size("dp")
    frames = rows * tm
    wide = rows + 2 * EDGE
    stacked = rows + rows // 2
    chunk = expert_in.shape[1]
    bf = lambda *shape: pltpu.VMEM(shape, BF)
    out = pl.pallas_call(
        functools.partial(block_kernel, tm, dp),
        out_shape=jax.ShapeDtypeStruct((rows, D), BF),
        in_specs=[smem_spec()] * 2 + [vmem_spec()] * 3 + [any_spec()] * 2 + [vmem_spec()] * 2 + [any_spec()] * 2,
        out_specs=vmem_spec(),
        scratch_shapes=[
            bf(tm, stacked, 128),
            bf(tm, stacked, 128),
            bf(frames, 128),
            bf(frames, 128),
            bf(frames, 128),
            bf(frames + 2 * EDGE, 128),
            bf(tm, wide // 2, 128),
            bf(tm, wide // 2, 128),
            pltpu.VMEM((wide, D), F32),
            pltpu.VMEM((D // 128, wide, 128), F32),
            pltpu.VMEM((wide, 128), jnp.int32),
            pltpu.VMEM((rows, D), F32),
            bf(dp, CAP_PAD, D),
            bf(dp, CAP_PAD, D),
            bf(tm, chunk, D),
            bf(tm, chunk, D),
            bf(dp * CAP_PAD, tm * chunk),
            bf(dp, CAP_PAD, D),
            bf(dp, CAP_PAD, D),
            bf(dp * CAP_PAD, rows),
            bf(TOPK, rows, dp * CAP_PAD),
            pltpu.VMEM((TOPK, dp, rows), F32),
            pltpu.VMEM((8, rows), F32),
            bf(*out_proj.shape),
            pltpu.VMEM(conv_taps.shape, F32),
        ]
        + sems(GATHER_IDS)
        + [pltpu.SemaphoreType.DMA((4,))]
        + sems(tm - 1)
        + [pltpu.SemaphoreType.DMA]
        + sems(tm - 1)
        + sems(dp - 1)
        + [pltpu.SemaphoreType.DMA]
        + sems(dp - 1),
        compiler_params=pltpu.CompilerParams(
            vmem_limit_bytes=VMEM_LIMIT, collective_id=0, has_side_effects=True
        ),
        name="block",
    )(
        head_scale,
        lengths,
        query_rows[0],
        key_rows[0],
        value_rows[0],
        out_proj,
        conv_taps,
        router.T,
        routes[0].T,
        expert_in,
        expert_out,
    )
    return out[None]


def solution(mesh):
    return jax.shard_map(
        body,
        mesh=mesh,
        in_specs=(
            P("dp", "tm", None),
            P("dp", "tm", None),
            P("dp", "tm", None),
            P(),
            P(),
            P(),
            P(),
            P("dp", "tm", None),
            P("dp", "tm", None),
            P("dp", None),
            P("dp", "tm", None),
        ),
        out_specs=P("dp", "tm", None),
        check_vma=False,
    )
```
